32 devices in a mesh: seq: 8 (over y, x, core), tp: 4 (over z).
Axes of the slice: x: 2, y: 2, z: 4, core: 2. Of those that a mesh axis runs over, the one named last changes fastest.
Arguments:
- hidden: bfloat16 [5120, 2048], P('seq', 'tp'), may hold values from -12 to 12
- w_qkv: bfloat16 [3, 2048, 2048], P(None, None, 'tp')
- w_out: bfloat16 [2048, 2048], P('tp'), may hold values from -0.125 to 0.125
- seg_ids: int32 [5120], P('seq'), may hold values from 0 to 16, as said below
- positions: int32 [5120], P('seq'), may hold values from 0 to 4095, as said below
- page_table: int32 [320], P('seq'), may hold values from 0 to 319, as said below
Outputs:
- delta: bfloat16 [5120, 2048], P('seq', 'tp')
- k_cache: bfloat16 [320, 16, 2048], P('seq', None, 'tp')
- v_cache: bfloat16 [320, 16, 2048], P('seq', None, 'tp')
The draws below stay inside these ranges and needn't reach their ends.
Inputs may be any that keep to these rules, and one draw needn't show every extreme that they name: `seg_ids`: tokens 0 to 4095 form prompt 0; the remaining tokens form prompts 1 to 16 in order, each of 16 to 112 tokens. `positions`: positions rise by one from token to token inside a prompt; prompt 0 starts at 0, every other prompt at a value below 256. `page_table`: every page appears once; page p lives on index p // 40 of seq; the pages of one index of seq go to at most 5 pages of any one owner, and exactly 5 to some owner.
All inputs are finite; a program needn't handle non-finite values.
Results may differ from the reference program's by a relative error of at most 0.0076.
Values may be sent and summed in bfloat16 or wider, within the bound.
A program may use at most 320 MiB of HBM per device.

```python
import math
import jax
import jax.numpy as jnp
from jax import lax

D = 2048
HEADS = 16
HEAD_DIM = 128
PAGE = 16
TOK_DEV = 640
TOKENS = 5120
LONG = 4096
SHORTS = 16
PAGES = 320
BLOCKS_DEV = 40


def short_layout(key):
    inner_key = jax.random.fold_in(key, 5)
    jitter = jax.random.randint(inner_key, (SHORTS,), -24, 25)
    cut_index = jnp.arange(SHORTS, dtype=jnp.int32)
    starts = LONG + 64 * cut_index + jnp.where(cut_index > 0, jitter, 0)
    token_index = jnp.arange(TOKENS, dtype=jnp.int32)
    segment = jnp.sum((token_index[:, None] >= starts[None, :]).astype(jnp.int32), axis=1)
    offsets = jax.random.randint(jax.random.fold_in(key, 6), (SHORTS,), 0, 256)
    start_table = jnp.concatenate([jnp.zeros((1,), jnp.int32), starts.astype(jnp.int32)])
    offset_table = jnp.concatenate([jnp.zeros((1,), jnp.int32), offsets.astype(jnp.int32)])
    position = token_index - start_table[segment] + offset_table[segment]
    return (segment.astype(jnp.int32), position.astype(jnp.int32))


def draw_seg_ids(key, part):
    return short_layout(key)[0]


def draw_positions(key, part):
    return short_layout(key)[1]


def draw_page_table(key, part):
    devices = PAGES // BLOCKS_DEV
    rotation = jax.random.randint(jax.random.fold_in(key, 21), (), 0, devices)
    order_keys = jax.random.split(jax.random.fold_in(key, 22), devices)
    order = jax.vmap(lambda one_key: jax.random.permutation(one_key, BLOCKS_DEV))(order_keys).astype(jnp.int32)
    source = jnp.arange(devices, dtype=jnp.int32)[:, None]
    owner = (source + (order + rotation) % devices) % devices
    occurrence = order // devices
    quotient = BLOCKS_DEV // devices
    remainder = BLOCKS_DEV % devices
    owner_index = jnp.arange(devices, dtype=jnp.int32)[None, :]
    counts = quotient + ((owner_index - source - rotation) % devices < remainder).astype(jnp.int32)
    earlier = jnp.cumsum(counts, axis=0) - counts
    source_full = jnp.broadcast_to(source, owner.shape)
    slot = earlier[source_full, owner] + occurrence
    shuffle_keys = jax.random.split(jax.random.fold_in(key, 23), devices)
    shuffle = jax.vmap(lambda one_key: jax.random.permutation(one_key, BLOCKS_DEV))(shuffle_keys).astype(jnp.int32)
    page = owner * BLOCKS_DEV + shuffle[owner, slot]
    return page.reshape(PAGES).astype(jnp.int32)


def draw_hidden(key, part):
    column_scale = jnp.exp(jax.random.uniform(jax.random.fold_in(key, 31), (D,), jnp.float32, 0.0, math.log(10.0)))
    regions = jax.random.normal(jax.random.fold_in(key, 32), (TOKENS // 128 + 1, D), jnp.float32)
    token_index = jnp.arange(TOKENS)
    region_part = regions[token_index // 128]
    noise = jax.random.normal(jax.random.fold_in(key, 33), (TOKENS, D), jnp.float32)
    offset = 0.5 * jax.random.normal(jax.random.fold_in(key, 34), (TOKENS, 1), jnp.float32)
    base = 0.5 * noise * column_scale[None, :] + region_part + offset
    return jnp.clip(base, -12.0, 12.0).astype(jnp.bfloat16)


def draw_w_qkv(key, part):
    spread = D ** (-0.5)
    base = jnp.clip(jax.random.normal(jax.random.fold_in(key, 11), (3, D, D), jnp.float32), -4.5, 4.5) * spread
    return base.astype(jnp.bfloat16)


def block_scale(key, extent, pieces, low, largest):
    def one(dim, shards_of):
        steps = jax.random.uniform(jax.random.fold_in(jax.random.fold_in(key, 6), dim), (shards_of,), jnp.float32, low / len(pieces), largest / len(pieces))
        return jnp.repeat(jnp.exp(steps), extent[dim] // shards_of).reshape((-1,) + (1,) * (len(extent) - dim - 1))

    loudness = one(*pieces[0])
    for cut in pieces[1:]:
        loudness = loudness * one(*cut)
    return loudness


def normal_values(stream_key, extent, width, most, cuts=(), kind=jnp.bfloat16):
    loudness = block_scale(stream_key, extent, cuts, -0.22, 0.18) if cuts else 1.0
    entries = jax.random.normal(stream_key, extent, jnp.float32) * width * loudness
    return jnp.minimum(jnp.maximum(entries, -most), most).astype(kind)


def setup_inputs(seed: int = 0) -> dict:
    seeds = jax.random.split(jax.random.key(seed), 7)
    return {
        "hidden": draw_hidden(jax.random.fold_in(seeds[6], 71), 0),
        "w_qkv": draw_w_qkv(jax.random.fold_in(seeds[6], 71), 0),
        "w_out": normal_values(seeds[2], (D, D), D ** -0.5, 0.125, ((0, 4),)),
        "seg_ids": draw_seg_ids(jax.random.fold_in(seeds[6], 71), 0),
        "positions": draw_positions(jax.random.fold_in(seeds[6], 71), 0),
        "page_table": draw_page_table(jax.random.fold_in(seeds[6], 71), 0),
    }


ROPE_BASE = 10000.0
EPSILON = 1e-05
NEG_LARGE = -1e+30

def rope_tables(position_ids, head_width):
    half_width = head_width // 2
    frequency = ROPE_BASE ** (-jnp.arange(half_width).astype(jnp.float32) * 2.0 / head_width)
    angle = position_ids.astype(jnp.float32)[:, None] * frequency[None, :]
    return (jnp.cos(angle), jnp.sin(angle))

def rotate(vectors, cosine, sine_part):
    half_width = vectors.shape[-1] // 2
    first_half = vectors[..., :half_width]
    second_half = vectors[..., half_width:]
    cos_rows = cosine[:, None, :]
    sin_rows = sine_part[:, None, :]
    return jnp.concatenate([first_half * cos_rows - second_half * sin_rows, second_half * cos_rows + first_half * sin_rows], axis=-1)

def reference(hidden, w_qkv, w_out, seg_ids, positions, page_table):
    tok_rows = hidden.astype(jnp.float32)
    row_mean = lax.optimization_barrier(jnp.mean(tok_rows, axis=1, keepdims=True))
    centred = tok_rows - row_mean
    row_var = lax.optimization_barrier(jnp.mean(centred * centred, axis=1, keepdims=True))
    normed = (centred * lax.rsqrt(row_var + EPSILON)).astype(jnp.bfloat16)
    projected = [jnp.dot(normed, w_qkv[index], preferred_element_type=jnp.float32) for index in range(3)]
    cosine, sine_part = rope_tables(positions, HEAD_DIM)
    queries = rotate(projected[0].reshape(TOKENS, HEADS, HEAD_DIM), cosine, sine_part).astype(jnp.bfloat16)
    key_heads = rotate(projected[1].reshape(TOKENS, HEADS, HEAD_DIM), cosine, sine_part).astype(jnp.bfloat16)
    values = projected[2].astype(jnp.bfloat16)
    key_wide = key_heads.astype(jnp.float32)
    value_wide = values.reshape(TOKENS, HEADS, HEAD_DIM).astype(jnp.float32)
    score_scale = HEAD_DIM ** (-0.5)
    block_rows = 256 if TOKENS % 256 == 0 else TOK_DEV
    block_count = TOKENS // block_rows

    def attend_block(operands):
        query_block, seg_block, pos_block = operands
        scores = jnp.einsum('qhe,khe->qhk', query_block.astype(jnp.float32), key_wide) * score_scale
        visible = (seg_ids[None, :] == seg_block[:, None]) & (positions[None, :] <= pos_block[:, None])
        scores = jnp.where(visible[:, None, :], scores, NEG_LARGE)
        row_max = lax.optimization_barrier(jnp.max(scores, axis=2, keepdims=True))
        weights = jnp.where(visible[:, None, :], jnp.exp(scores - row_max), 0.0)
        weight_sum = lax.optimization_barrier(jnp.sum(weights, axis=2))
        probs = lax.optimization_barrier(weights.astype(jnp.bfloat16)).astype(jnp.float32)
        mixed = jnp.einsum('qhk,khe->qhe', probs, value_wide)
        return (mixed / weight_sum[:, :, None]).astype(jnp.bfloat16)
    attended = lax.map(attend_block, (queries.reshape(block_count, block_rows, HEADS, HEAD_DIM), seg_ids.reshape(block_count, block_rows), positions.reshape(block_count, block_rows)))
    attended = attended.reshape(TOKENS, D)
    delta = jnp.dot(attended, w_out, preferred_element_type=jnp.float32).astype(jnp.bfloat16)
    key_pages = key_heads.reshape(PAGES, PAGE, D)
    value_pages = values.reshape(PAGES, PAGE, D)
    k_cache = jnp.zeros((PAGES, PAGE, D), jnp.bfloat16).at[page_table].set(key_pages)
    v_cache = jnp.zeros((PAGES, PAGE, D), jnp.bfloat16).at[page_table].set(value_pages)
    return (delta, k_cache, v_cache)
```

```python
import functools
import math

import jax
import jax.numpy as jnp
from jax import lax
from jax.sharding import PartitionSpec as P
from jax.experimental import pallas as pl
from jax.experimental.pallas import tpu as pltpu

HEAD_DIM = 128
PAGE = 16
ROPE_BASE = 10000.0
EPSILON = 1e-05
NEG_LARGE = -1e30
SCALE = HEAD_DIM ** -0.5 * math.log2(math.e)
MESH = pl.DeviceIdType.MESH
CHUNK = 128
STRADDLE = 128


def flip(index, bit):
    return index + (1 << bit) * (1 - 2 * ((index // (1 << bit)) % 2))


def flips(index, bits):
    found = [index]
    for bit in bits:
        found = found + [flip(one, bit) for one in found]
    return found


def sublayer_kernel(seqs, tps, long_rows,
                    hid, wqkv, wout, cos2, sin2, ints,
                    delta, kv_out, ints_all,
                    wq_s, wo_s, hfull, q_s, kv, m_s, l_s, acc_s, att_s, part, sendbuf, from_left, from_right,
                    z_send, z_recv, kv_send, kv_recv, int_send, int_recv, rs_send, rs_recv, local_sem, out_sem):
    me = lax.axis_index("seq")
    z = lax.axis_index("tp")
    core, chip = me % 2, me // 2
    chips = seqs // 2
    chip_bits = chips.bit_length() - 1
    rows_dev, width = hid.shape
    heads = width // HEAD_DIM
    chunks = rows_dev // CHUNK
    split = long_rows % rows_dev

    barrier = pltpu.get_barrier_semaphore()
    for bit in range(chip_bits + 1):
        pl.semaphore_signal(barrier, inc=1, device_id={"seq": flip(me, bit)}, device_id_type=MESH)

    @pl.when(z > 0)
    def _():
        pl.semaphore_signal(barrier, inc=1, device_id={"tp": z - 1}, device_id_type=MESH)

    @pl.when(z < tps - 1)
    def _():
        pl.semaphore_signal(barrier, inc=1, device_id={"tp": z + 1}, device_id_type=MESH)

    load_h = pltpu.make_async_copy(hid, hfull.at[z], local_sem.at[0])
    load_q = pltpu.make_async_copy(wqkv, wq_s, local_sem.at[1])
    load_o = pltpu.make_async_copy(wout, wo_s, local_sem.at[2])
    load_h.start()
    load_q.start()
    load_o.start()
    neighbours = (z > 0).astype(jnp.int32) + (z < tps - 1).astype(jnp.int32)
    pl.semaphore_wait(barrier, chip_bits + 1 + neighbours)

    def chunk_rows(c):
        return pl.ds(c * CHUNK, CHUNK)

    def z_copy(way, hop, c):
        shard = z - way * (hop - 1)
        source = hid.at[chunk_rows(c)] if hop == 1 else hfull.at[shard, chunk_rows(c)]
        side = 0 if way > 0 else 1
        return pltpu.make_async_remote_copy(
            src_ref=source, dst_ref=hfull.at[shard, chunk_rows(c)],
            send_sem=z_send.at[side, hop, c], recv_sem=z_recv.at[side, hop, c],
            device_id={"tp": z + way}, device_id_type=MESH)

    def has(way, hop):
        ahead = z + 1 < tps if way > 0 else z > 0
        held = z - (hop - 1) >= 0 if way > 0 else z + (hop - 1) < tps
        return ahead & held

    def gets(way, hop):
        return z - hop >= 0 if way > 0 else z + hop < tps

    def z_start(way, hop, c):
        @pl.when(has(way, hop))
        def _():
            z_copy(way, hop, c).start()

    def z_arrive(way, hop, c):
        @pl.when(gets(way, hop))
        def _():
            z_copy(way, hop, c).wait_recv()

    def z_pass(c):
        for hop in range(1, tps):
            for way in (1, -1):
                z_arrive(way, hop, c)
                if hop + 1 < tps:
                    z_start(way, hop + 1, c)

    orders = (list(range(chip_bits)), list(range(chip_bits))[::-1])
    half = CHUNK // 2

    def kv_copies(stage, c):
        found = []
        if stage == chip_bits:
            found.append((kv.at[core, :, chunk_rows(c)], {"seq": flip(me, 0)}))
        else:
            for side, order in enumerate(orders):
                rows = pl.ds(c * CHUNK + side * half, half)
                to = flip(chip, order[stage]) * 2 + core
                for shard in flips(chip, order[:stage]):
                    found.append((kv.at[core, shard, rows], {"seq": to}))
        base = sum(2 << s for s in range(stage))
        return [
            pltpu.make_async_remote_copy(
                src_ref=ref, dst_ref=ref, send_sem=kv_send.at[c, base + k], recv_sem=kv_recv.at[c, base + k],
                device_id=to, device_id_type=MESH)
            for k, (ref, to) in enumerate(found)
        ]

    def kv_start(stage, c):
        for copy in kv_copies(stage, c):
            copy.start()

    def kv_arrive(stage, c):
        for copy in kv_copies(stage, c):
            copy.wait_recv()

    def kv_store(c):
        return pltpu.make_async_copy(
            kv.at[:, :, chunk_rows(c)], kv_out.at[:, :, chunk_rows(c)], out_sem.at[c])

    for way in (1, -1):
        z_start(way, 1, 0)
    for way in (1, -1):
        z_start(way, 1, 1)

    ints_all[me] = ints[...]
    for bit in range(chip_bits + 1):
        first = (me // (1 << bit)) * (1 << bit)
        copy = pltpu.make_async_remote_copy(
            src_ref=ints_all.at[pl.ds(first, 1 << bit)], dst_ref=ints_all.at[pl.ds(first, 1 << bit)],
            send_sem=int_send.at[bit], recv_sem=int_recv.at[bit],
            device_id={"seq": flip(me, bit)}, device_id_type=MESH)
        copy.start()
        copy.wait()

    load_h.wait()
    load_q.wait()

    def project(c):
        rows = chunk_rows(c)
        pieces = [hfull[t, rows, :].astype(jnp.float32) for t in range(tps)]
        total = sum(jnp.sum(piece, axis=1, keepdims=True) for piece in pieces)
        mean = total * (1.0 / (tps * width))
        centred = [piece - mean for piece in pieces]
        spread = sum(jnp.sum(piece * piece, axis=1, keepdims=True) for piece in centred)
        factor = lax.rsqrt(spread * (1.0 / (tps * width)) + EPSILON)
        normed = jnp.concatenate([(piece * factor).astype(jnp.bfloat16) for piece in centred], axis=1)
        cos, sin = cos2[rows, :], sin2[rows, :]
        for which in range(3):
            projected = jnp.dot(normed, wq_s[which], preferred_element_type=jnp.float32)
            for h in range(heads):
                part_h = projected[:, h * HEAD_DIM:(h + 1) * HEAD_DIM]
                if which < 2:
                    part_h = part_h * cos + pltpu.roll(part_h, HEAD_DIM // 2, 1) * sin
                value = part_h.astype(jnp.bfloat16)
                if which == 0:
                    q_s[rows, h * HEAD_DIM:(h + 1) * HEAD_DIM] = value
                else:
                    at = (which - 1) * width + h * HEAD_DIM
                    kv[core, chip, rows, at:at + HEAD_DIM] = value

    for c in range(chunks + chip_bits + 1):
        if c < chunks:
            if c + 2 < chunks:
                for way in (1, -1):
                    z_start(way, 1, c + 2)
            z_pass(c)
            project(c)
            kv_start(0, c)
        for stage in range(chip_bits + 1):
            older = c - 1 - stage
            if 0 <= older < chunks:
                kv_arrive(stage, older)
                if stage < chip_bits:
                    kv_start(stage + 1, older)
                else:
                    kv_store(older).start()

    tiles = [(0, split), (split, rows_dev)] if split else [(0, rows_dev)]

    def seg_row(device):
        return [ints_all[device, r:r + 1, :] for r in range(rows_dev // 128)]

    def as_column(row):
        return jnp.transpose(jnp.broadcast_to(row.astype(jnp.float32), (128, 128)))[:, :1]

    def unit(key_at, h, tile, mask, first):
        low, high = tile
        cols = pl.ds(h * HEAD_DIM, HEAD_DIM)
        keys = kv[key_at + (cols,)]
        values = kv[key_at + (pl.ds(width + h * HEAD_DIM, HEAD_DIM),)]
        s = lax.dot_general(keys, q_s[low:high, h * HEAD_DIM:(h + 1) * HEAD_DIM], (((1,), (1,)), ((), ())),
                            preferred_element_type=jnp.float32)
        if mask is not None:
            s = jnp.where(mask, s, NEG_LARGE)
        top = jnp.max(s, axis=0, keepdims=True)
        if not first:
            before = m_s[h, :, low:high]
            top = jnp.maximum(top, before)
        p = jnp.exp2((s - top) * SCALE)
        total = jnp.sum(p, axis=0, keepdims=True)
        mixed = lax.dot_general(values, p.astype(jnp.bfloat16), (((0,), (0,)), ((), ())),
                                preferred_element_type=jnp.float32)
        if not first:
            alpha = jnp.exp2((before - top) * SCALE)
            total = total + alpha * l_s[h, :, low:high]
            mixed = mixed + alpha * acc_s[h, :, low:high]
        m_s[h, :, low:high] = top
        l_s[h, :, low:high] = total
        acc_s[h, :, low:high] = mixed

    own = seg_row(me)
    own_row = jnp.concatenate(own, axis=1).astype(jnp.float32)
    own_col = jnp.concatenate([as_column(row) for row in own], axis=0)
    for low, high in tiles:
        key_index = lax.broadcasted_iota(jnp.int32, (high, high - low), 0)
        query_index = lax.broadcasted_iota(jnp.int32, (high, high - low), 1) + low
        mask = (own_col[:high] == own_row[:, low:high]) & (key_index <= query_index)
        for h in range(heads):
            unit((core, chip, pl.ds(0, high)), h, (low, high), mask, True)

    starts_long = me * rows_dev < long_rows
    all_long = (me + 1) * rows_dev <= long_rows

    def attend_device(j, carry):
        at = (j % 2, j // 2, pl.ds(0, rows_dev))
        for h in range(heads):
            unit(at, h, tiles[0], None, False)
        if len(tiles) > 1:
            @pl.when(all_long)
            def _():
                for h in range(heads):
                    unit(at, h, tiles[1], None, False)
        return carry

    lax.fori_loop(0, jnp.where(starts_long, me, 0), attend_device, 0)

    @pl.when(jnp.logical_not(starts_long))
    def _():
        before = me - 1
        row = ints_all[before, rows_dev // 128 - 1:rows_dev // 128, :]
        low, high = tiles[0]
        mask = as_column(row) == own_row[:, low:high]
        for h in range(heads):
            unit((before % 2, before // 2, pl.ds(rows_dev - STRADDLE, STRADDLE)), h, tiles[0], mask, False)

    for h in range(heads):
        att_s[h * HEAD_DIM:(h + 1) * HEAD_DIM, :] = (acc_s[h] / l_s[h]).astype(jnp.bfloat16)

    load_o.wait()

    def rs_copy(way, j, c):
        landing = from_left if way > 0 else from_right
        side = 0 if way > 0 else 1
        return pltpu.make_async_remote_copy(
            src_ref=sendbuf.at[j, chunk_rows(c)], dst_ref=landing.at[j, chunk_rows(c)],
            send_sem=rs_send.at[j, c], recv_sem=rs_recv.at[side, j, c],
            device_id={"tp": z + way}, device_id_type=MESH)

    ways = {1: list(range(tps - 1, 0, -1)), -1: list(range(0, tps - 1))}
    for c in range(chunks):
        rows = chunk_rows(c)
        for j in range(tps):
            part[j, rows, :] = lax.dot_general(
                att_s[:, c * CHUNK:(c + 1) * CHUNK], wo_s[:, j * width:(j + 1) * width], (((0,), (0,)), ((), ())),
                preferred_element_type=jnp.float32)
        for way in (1, -1):
            @pl.when(z == (0 if way > 0 else tps - 1))
            def _():
                for j in ways[way]:
                    sendbuf[j, rows, :] = part[j, rows, :].astype(jnp.bfloat16)
                    rs_copy(way, j, c).start()

    for c in range(chunks):
        rows = chunk_rows(c)
        for hop in range(1, tps - 1):
            for way in (1, -1):
                landing = from_left if way > 0 else from_right

                @pl.when(z == (hop if way > 0 else tps - 1 - hop))
                def _():
                    for j in ways[way]:
                        if (j > hop) if way > 0 else (j < tps - 1 - hop):
                            rs_copy(way, j, c).wait_recv()
                            sendbuf[j, rows, :] = (
                                part[j, rows, :] + landing[j, rows, :].astype(jnp.float32)).astype(jnp.bfloat16)
                            rs_copy(way, j, c).start()

        @pl.when(z > 0)
        def _():
            rs_copy(1, z, c).wait_recv()
            part[z, rows, :] = part[z, rows, :] + from_left[z, rows, :].astype(jnp.float32)

        @pl.when(z < tps - 1)
        def _():
            rs_copy(-1, z, c).wait_recv()
            part[z, rows, :] = part[z, rows, :] + from_right[z, rows, :].astype(jnp.float32)

        delta[rows, :] = part[z, rows, :].astype(jnp.bfloat16)

    for c in range(chunks):
        for way in (1, -1):
            for hop in range(1, tps):
                @pl.when(has(way, hop))
                def _():
                    z_copy(way, hop, c).wait_send()
        for stage in range(chip_bits + 1):
            for copy in kv_copies(stage, c):
                copy.wait_send()
        kv_store(c).wait()
        for j in range(tps):
            @pl.when(z != j)
            def _():
                rs_copy(1, j, c).wait_send()


def page_kernel(blocks_dev, table, kv, k_cache, v_cache, sem):
    me = lax.axis_index("seq")
    seqs = table.shape[0]
    width = k_cache.shape[2]
    row = table.shape[1] - 3

    def copies(source, page):
        device, block = source // blocks_dev, source % blocks_dev
        rows = kv.at[device % 2, device // 2, pl.ds(pl.multiple_of(block * PAGE, PAGE), PAGE)]
        return (
            pltpu.make_async_copy(rows.at[:, pl.ds(0, width)], k_cache.at[page], sem.at[0]),
            pltpu.make_async_copy(rows.at[:, pl.ds(width, width)], v_cache.at[page], sem.at[1]),
        )

    def scan(source, carry):
        page = table[source // blocks_dev, row, source % blocks_dev] - me * blocks_dev

        @pl.when((page >= 0) & (page < blocks_dev))
        def _():
            for copy in copies(source, page):
                copy.start()
        return carry

    lax.fori_loop(0, seqs * blocks_dev, scan, 0)
    pltpu.make_async_copy(k_cache, k_cache, sem.at[0]).wait()
    pltpu.make_async_copy(v_cache, v_cache, sem.at[1]).wait()


def body(seqs, tps, hidden, w_qkv, w_out, seg_ids, positions, page_table):
    rows, width = hidden.shape
    heads = width // HEAD_DIM
    chips = seqs // 2
    chip_bits = chips.bit_length() - 1
    chunks = rows // CHUNK
    blocks_dev = page_table.shape[0]
    long_rows = seqs * rows * 4 // 5
    half = HEAD_DIM // 2
    frequency = ROPE_BASE ** (-jnp.arange(half).astype(jnp.float32) * 2.0 / HEAD_DIM)
    angle = positions.astype(jnp.float32)[:, None] * frequency[None, :]
    cosine, sine = jnp.cos(angle), jnp.sin(angle)
    cos2 = jnp.concatenate([cosine, cosine], axis=1)
    sin2 = jnp.concatenate([-sine, sine], axis=1)
    seg_rows = rows // 128
    ints = jnp.concatenate([seg_ids, jnp.pad(page_table, (0, 3 * 128 - blocks_dev))]).reshape(seg_rows + 3, 128)
    anywhere = pl.BlockSpec(memory_space=pl.ANY)
    vmem = pl.BlockSpec(memory_space=pltpu.VMEM)
    kv_stage_copies = sum(2 << s for s in range(chip_bits)) + 1
    bf16, f32 = jnp.bfloat16, jnp.float32
    dma = pltpu.SemaphoreType.DMA
    delta, kv_all, ints_all = pl.pallas_call(
        functools.partial(sublayer_kernel, seqs, tps, long_rows),
        out_shape=(
            jax.ShapeDtypeStruct((rows, width), bf16),
            jax.ShapeDtypeStruct((2, chips, rows, 2 * width), bf16),
            jax.ShapeDtypeStruct((seqs, seg_rows + 3, 128), jnp.int32),
        ),
        in_specs=[anywhere, anywhere, anywhere, vmem, vmem, vmem],
        out_specs=(vmem, anywhere, vmem),
        scratch_shapes=[
            pltpu.VMEM(w_qkv.shape, bf16),
            pltpu.VMEM(w_out.shape, bf16),
            pltpu.VMEM((tps, rows, width), bf16),
            pltpu.VMEM((rows, width), bf16),
            pltpu.VMEM((2, chips, rows, 2 * width), bf16),
            pltpu.VMEM((heads, 1, rows), f32),
            pltpu.VMEM((heads, 1, rows), f32),
            pltpu.VMEM((heads, HEAD_DIM, rows), f32),
            pltpu.VMEM((width, rows), bf16),
            pltpu.VMEM((tps, rows, width), f32),
            pltpu.VMEM((tps, rows, width), bf16),
            pltpu.VMEM((tps, rows, width), bf16),
            pltpu.VMEM((tps, rows, width), bf16),
            dma((2, tps, chunks)), dma((2, tps, chunks)),
            dma((chunks, kv_stage_copies)), dma((chunks, kv_stage_copies)),
            dma((chip_bits + 1,)), dma((chip_bits + 1,)),
            dma((tps, chunks)), dma((2, tps, chunks)),
            dma((3,)), dma((chunks,)),
        ],
        compiler_params=pltpu.CompilerParams(
            collective_id=0, has_side_effects=True, vmem_limit_bytes=60 * 1024 * 1024),
    )(hidden, w_qkv, w_out, cos2, sin2, ints)
    k_cache, v_cache = pl.pallas_call(
        functools.partial(page_kernel, blocks_dev),
        out_shape=(jax.ShapeDtypeStruct((blocks_dev, PAGE, width), bf16),) * 2,
        in_specs=[pl.BlockSpec(memory_space=pltpu.SMEM), anywhere],
        out_specs=(anywhere, anywhere),
        scratch_shapes=[dma((2,))],
    )(ints_all, kv_all)
    return delta, k_cache, v_cache


def solution(mesh):
    in_specs = (P("seq", "tp"), P(None, None, "tp"), P("tp", None), P("seq"), P("seq"), P("seq"))
    out_specs = (P("seq", "tp"), P("seq", None, "tp"), P("seq", None, "tp"))
    return jax.shard_map(
        functools.partial(body, mesh.shape["seq"], mesh.shape["tp"]),
        mesh=mesh, in_specs=in_specs, out_specs=out_specs, check_vma=False)
```

```python
import functools
import math

import jax
import jax.numpy as jnp
from jax import lax
from jax.sharding import PartitionSpec as P
from jax.experimental import pallas as pl
from jax.experimental.pallas import tpu as pltpu

HEAD_DIM = 128
PAGE = 16
ROPE_BASE = 10000.0
EPSILON = 1e-05
NEG_LARGE = -1e30
SCALE = HEAD_DIM ** -0.5 * math.log2(math.e)
MESH = pl.DeviceIdType.MESH
CHUNK = 128
STRADDLE = 128


def row_sizes(rows):
    return [64] + [128] * (rows // 128 - 1) + [64]


def flip(index, bit):
    return index + (1 << bit) * (1 - 2 * ((index // (1 << bit)) % 2))


def flips(index, bits):
    found = [index]
    for bit in bits:
        found = found + [flip(one, bit) for one in found]
    return found


def sublayer_kernel(seqs, tps, long_rows,
                    hid, wqkv, wout, cos2, sin2, ints,
                    delta, kv_out, ints_all,
                    wq_s, wo_s, hfull, q_s, kv, m_s, l_s, acc_s, att_s, part, sendbuf, from_left, from_right,
                    z_send, z_recv, kv_send, kv_recv, int_send, int_recv, rs_send, rs_recv, local_sem, out_sem):
    me = lax.axis_index("seq")
    z = lax.axis_index("tp")
    core, chip = me % 2, me // 2
    chips = seqs // 2
    chip_bits = chips.bit_length() - 1
    rows_dev, width = hid.shape
    heads = width // HEAD_DIM
    sizes = row_sizes(rows_dev)
    offsets = [sum(sizes[:c]) for c in range(len(sizes))]
    chunks = len(sizes)
    steps = rows_dev // CHUNK
    split = long_rows % rows_dev

    barrier = pltpu.get_barrier_semaphore()
    for bit in range(chip_bits + 1):
        pl.semaphore_signal(barrier, inc=1, device_id={"seq": flip(me, bit)}, device_id_type=MESH)

    @pl.when(z > 0)
    def _():
        pl.semaphore_signal(barrier, inc=1, device_id={"tp": z - 1}, device_id_type=MESH)

    @pl.when(z < tps - 1)
    def _():
        pl.semaphore_signal(barrier, inc=1, device_id={"tp": z + 1}, device_id_type=MESH)

    load_h = pltpu.make_async_copy(hid, hfull.at[z], local_sem.at[0])
    load_q = pltpu.make_async_copy(wqkv, wq_s, local_sem.at[1])
    load_o = pltpu.make_async_copy(wout, wo_s, local_sem.at[2])
    load_h.start()
    load_q.start()
    load_o.start()
    neighbours = (z > 0).astype(jnp.int32) + (z < tps - 1).astype(jnp.int32)
    pl.semaphore_wait(barrier, chip_bits + 1 + neighbours)

    def chunk_rows(c):
        return pl.ds(offsets[c], sizes[c])

    def z_copy(way, hop, c):
        shard = z - way * (hop - 1)
        source = hid.at[chunk_rows(c)] if hop == 1 else hfull.at[shard, chunk_rows(c)]
        side = 0 if way > 0 else 1
        return pltpu.make_async_remote_copy(
            src_ref=source, dst_ref=hfull.at[shard, chunk_rows(c)],
            send_sem=z_send.at[side, hop, c], recv_sem=z_recv.at[side, hop, c],
            device_id={"tp": z + way}, device_id_type=MESH)

    def has(way, hop):
        ahead = z + 1 < tps if way > 0 else z > 0
        held = z - (hop - 1) >= 0 if way > 0 else z + (hop - 1) < tps
        return ahead & held

    def gets(way, hop):
        return z - hop >= 0 if way > 0 else z + hop < tps

    def z_start(way, hop, c):
        @pl.when(has(way, hop))
        def _():
            z_copy(way, hop, c).start()

    def z_arrive(way, hop, c):
        @pl.when(gets(way, hop))
        def _():
            z_copy(way, hop, c).wait_recv()

    def z_pass(hop, c):
        for way in (1, -1):
            z_arrive(way, hop, c)
            if hop + 1 < tps:
                z_start(way, hop + 1, c)

    orders = (list(range(chip_bits)), list(range(chip_bits))[::-1])
    def kv_copies(stage, c):
        found = []
        if stage == chip_bits:
            found.append((kv.at[core, :, chunk_rows(c)], {"seq": flip(me, 0)}))
        else:
            for side, order in enumerate(orders):
                half = sizes[c] // 2
                rows = pl.ds(offsets[c] + side * half, half)
                to = flip(chip, order[stage]) * 2 + core
                for shard in flips(chip, order[:stage]):
                    found.append((kv.at[core, shard, rows], {"seq": to}))
        base = sum(2 << s for s in range(stage))
        return [
            pltpu.make_async_remote_copy(
                src_ref=ref, dst_ref=ref, send_sem=kv_send.at[c, base + k], recv_sem=kv_recv.at[c, base + k],
                device_id=to, device_id_type=MESH)
            for k, (ref, to) in enumerate(found)
        ]

    def kv_start(stage, c):
        for copy in kv_copies(stage, c):
            copy.start()

    def kv_arrive(stage, c):
        for copy in kv_copies(stage, c):
            copy.wait_recv()

    def kv_store(c):
        return pltpu.make_async_copy(
            kv.at[:, :, chunk_rows(c)], kv_out.at[:, :, chunk_rows(c)], out_sem.at[c])

    for way in (1, -1):
        z_start(way, 1, 0)
    for way in (1, -1):
        z_start(way, 1, 1)

    ints_all[me] = ints[...]

    def ints_copy(bit):
        first = (me // (1 << bit)) * (1 << bit)
        block = ints_all.at[pl.ds(first, 1 << bit)]
        return pltpu.make_async_remote_copy(
            src_ref=block, dst_ref=block, send_sem=int_send.at[bit], recv_sem=int_recv.at[bit],
            device_id={"seq": flip(me, bit)}, device_id_type=MESH)

    ints_copy(0).start()
    load_h.wait()
    load_q.wait()

    def project(c):
        rows = chunk_rows(c)
        pieces = [hfull[t, rows, :].astype(jnp.float32) for t in range(tps)]
        total = sum(jnp.sum(piece, axis=1, keepdims=True) for piece in pieces)
        mean = total * (1.0 / (tps * width))
        centred = [piece - mean for piece in pieces]
        spread = sum(jnp.sum(piece * piece, axis=1, keepdims=True) for piece in centred)
        factor = lax.rsqrt(spread * (1.0 / (tps * width)) + EPSILON)
        normed = jnp.concatenate([(piece * factor).astype(jnp.bfloat16) for piece in centred], axis=1)
        cos, sin = cos2[rows, :], sin2[rows, :]
        for which in range(3):
            projected = jnp.dot(normed, wq_s[which], preferred_element_type=jnp.float32)
            for h in range(heads):
                part_h = projected[:, h * HEAD_DIM:(h + 1) * HEAD_DIM]
                if which < 2:
                    part_h = part_h * cos + pltpu.roll(part_h, HEAD_DIM // 2, 1) * sin
                value = part_h.astype(jnp.bfloat16)
                if which == 0:
                    q_s[rows, h * HEAD_DIM:(h + 1) * HEAD_DIM] = value
                else:
                    at = (which - 1) * width + h * HEAD_DIM
                    kv[core, chip, rows, at:at + HEAD_DIM] = value

    def kv_next(stage, c):
        if 0 <= c < chunks:
            kv_arrive(stage, c)
            if stage < chip_bits:
                kv_start(stage + 1, c)
            else:
                kv_store(c).start()

    for c in range(chunks):
        if c + 2 < chunks:
            for way in (1, -1):
                z_start(way, 1, c + 2)
        for hop in range(1, tps):
            z_pass(hop, c)
            if hop == 1:
                for stage in range(chip_bits - 1, 0, -1):
                    kv_next(stage, c - 1 - stage)
            if hop == 2:
                kv_next(0, c - 1)
        kv_next(chip_bits, c - chip_bits)
        if c <= chip_bits:
            ints_copy(c).wait()
            if c < chip_bits:
                ints_copy(c + 1).start()
        project(c)
        kv_start(0, c)
    if chunks <= chip_bits:
        for bit in range(chunks, chip_bits + 1):
            ints_copy(bit).wait()
            if bit < chip_bits:
                ints_copy(bit + 1).start()

    tiles = [(0, split), (split, rows_dev)] if split else [(0, rows_dev)]

    def seg_row(device):
        return [ints_all[device, r:r + 1, :] for r in range(rows_dev // 128)]

    def as_column(row):
        return jnp.transpose(jnp.broadcast_to(row.astype(jnp.float32), (128, 128)))[:, :1]

    def score(key_at, h, tile):
        low, high = tile
        return lax.dot_general(kv[key_at + (pl.ds(h * HEAD_DIM, HEAD_DIM),)],
                               q_s[low:high, h * HEAD_DIM:(h + 1) * HEAD_DIM], (((1,), (1,)), ((), ())),
                               preferred_element_type=jnp.float32)

    def absorb(s, key_at, h, tile, mask, first):
        low, high = tile
        values = kv[key_at + (pl.ds(width + h * HEAD_DIM, HEAD_DIM),)]
        if mask is not None:
            s = jnp.where(mask, s, NEG_LARGE)
        top = jnp.max(s, axis=0, keepdims=True)
        if not first:
            before = m_s[h, :, low:high]
            top = jnp.maximum(top, before)
        p = jnp.exp2((s - top) * SCALE)
        total = jnp.sum(p, axis=0, keepdims=True)
        mixed = lax.dot_general(values, p.astype(jnp.bfloat16), (((0,), (0,)), ((), ())),
                                preferred_element_type=jnp.float32)
        if not first:
            alpha = jnp.exp2((before - top) * SCALE)
            total = total + alpha * l_s[h, :, low:high]
            mixed = mixed + alpha * acc_s[h, :, low:high]
        m_s[h, :, low:high] = top
        l_s[h, :, low:high] = total
        acc_s[h, :, low:high] = mixed

    def attend(units, mask=None, first=False):
        ahead = score(*units[0])
        for k, one in enumerate(units):
            now = ahead
            if k + 1 < len(units):
                ahead = score(*units[k + 1])
            absorb(now, *one, mask, first)

    own = seg_row(me)
    own_row = jnp.concatenate(own, axis=1).astype(jnp.float32)
    own_col = jnp.concatenate([as_column(row) for row in own], axis=0)
    starts_long = me * rows_dev < long_rows
    all_long = (me + 1) * rows_dev <= long_rows

    def attend_own(tile):
        low, high = tile
        key_index = lax.broadcasted_iota(jnp.int32, (high, high - low), 0)
        query_index = lax.broadcasted_iota(jnp.int32, (high, high - low), 1) + low
        mask = (own_col[:high] == own_row[:, low:high]) & (key_index <= query_index)
        attend([((core, chip, pl.ds(0, high)), h, tile) for h in range(heads)], mask, True)

    def attend_before(which, rows):
        tile = tiles[which]

        def attend_device(j, carry):
            attend([((j % 2, j // 2, rows), h, tile) for h in range(heads)])
            return carry

        lax.fori_loop(0, jnp.where(starts_long if which == 0 else all_long, me, 0), attend_device, 0)

    def attend_straddle():
        @pl.when(jnp.logical_not(starts_long))
        def _():
            before = me - 1
            row = ints_all[before, rows_dev // 128 - 1:rows_dev // 128, :]
            low, high = tiles[0]
            mask = as_column(row) == own_row[:, low:high]
            at = (before % 2, before // 2, pl.ds(rows_dev - STRADDLE, STRADDLE))
            attend([(at, h, tiles[0]) for h in range(heads)], mask)

    def finish(tile):
        low, high = tile
        for h in range(heads):
            att_s[h * HEAD_DIM:(h + 1) * HEAD_DIM, low:high] = (
                acc_s[h, :, low:high] / l_s[h, :, low:high]).astype(jnp.bfloat16)

    def rs_copy(way, j, c):
        landing = from_left if way > 0 else from_right
        side = 0 if way > 0 else 1
        return pltpu.make_async_remote_copy(
            src_ref=sendbuf.at[j, step_rows(c)], dst_ref=landing.at[j, step_rows(c)],
            send_sem=rs_send.at[j, c], recv_sem=rs_recv.at[side, j, c],
            device_id={"tp": z + way}, device_id_type=MESH)

    ways = {1: list(range(tps - 1, 0, -1)), -1: list(range(0, tps - 1))}
    def step_rows(c):
        return pl.ds(c * CHUNK, CHUNK)

    def project_out(c):
        rows = step_rows(c)
        for j in range(tps):
            part[j, rows, :] = lax.dot_general(
                att_s[:, c * CHUNK:(c + 1) * CHUNK], wo_s[:, j * width:(j + 1) * width], (((0,), (0,)), ((), ())),
                preferred_element_type=jnp.float32)
        for way in (1, -1):
            @pl.when(z == (0 if way > 0 else tps - 1))
            def _():
                for j in ways[way]:
                    sendbuf[j, rows, :] = part[j, rows, :].astype(jnp.bfloat16)
                    rs_copy(way, j, c).start()

    last = chunks - 1
    early_rows = offsets[max(0, last - chip_bits + 1)]
    early, late = pl.ds(0, early_rows), pl.ds(early_rows, rows_dev - early_rows)
    work = [functools.partial(attend_own, tile) for tile in tiles]
    if early_rows:
        work += [functools.partial(attend_before, which, early) for which in range(len(tiles))]
    pending = [(c + min(stage + 1, chip_bits) + (stage == chip_bits) / 2, c, stage)
               for c in range(chunks) for stage in range(chip_bits + 1) if c + min(stage + 1, chip_bits) > last]
    pending = [(stage, c) for _, c, stage in sorted(pending)]
    places = (0, 1, len(pending) - 2, len(pending) - 1)
    for k, one in enumerate(pending):
        for place, task in zip(places, work):
            if place == k:
                task()
        kv_next(*one)
    load_o.wait()
    for which, tile in enumerate(tiles):
        attend_before(which, late)
        if which == 0:
            attend_straddle()
        finish(tile)
        for c in range(tile[0] // CHUNK, tile[1] // CHUNK):
            project_out(c)

    for c in range(steps):
        rows = step_rows(c)
        for hop in range(1, tps - 1):
            for way in (1, -1):
                landing = from_left if way > 0 else from_right

                @pl.when(z == (hop if way > 0 else tps - 1 - hop))
                def _():
                    for j in ways[way]:
                        if (j > hop) if way > 0 else (j < tps - 1 - hop):
                            rs_copy(way, j, c).wait_recv()
                            sendbuf[j, rows, :] = (
                                part[j, rows, :] + landing[j, rows, :].astype(jnp.float32)).astype(jnp.bfloat16)
                            rs_copy(way, j, c).start()

        @pl.when(z > 0)
        def _():
            rs_copy(1, z, c).wait_recv()
            part[z, rows, :] = part[z, rows, :] + from_left[z, rows, :].astype(jnp.float32)

        @pl.when(z < tps - 1)
        def _():
            rs_copy(-1, z, c).wait_recv()
            part[z, rows, :] = part[z, rows, :] + from_right[z, rows, :].astype(jnp.float32)

        delta[rows, :] = part[z, rows, :].astype(jnp.bfloat16)

    for c in range(chunks):
        for way in (1, -1):
            for hop in range(1, tps):
                @pl.when(has(way, hop))
                def _():
                    z_copy(way, hop, c).wait_send()
        for stage in range(chip_bits + 1):
            for copy in kv_copies(stage, c):
                copy.wait_send()
        kv_store(c).wait()
    for c in range(steps):
        for j in range(tps):
            @pl.when(z != j)
            def _():
                rs_copy(1, j, c).wait_send()


def page_kernel(blocks_dev, table, kv, k_cache, v_cache, sem):
    me = lax.axis_index("seq")
    seqs = table.shape[0]
    width = k_cache.shape[2]
    row = table.shape[1] - 3

    def copies(device, block, page):
        rows = kv.at[device % 2, device // 2, pl.ds(block * PAGE, PAGE)]
        return (
            pltpu.make_async_copy(rows.at[:, pl.ds(0, width)], k_cache.at[page], sem.at[0]),
            pltpu.make_async_copy(rows.at[:, pl.ds(width, width)], v_cache.at[page], sem.at[1]),
        )

    def scan(device, carry):
        for block in range(blocks_dev):
            page = table[device, row, block] - me * blocks_dev

            @pl.when((page >= 0) & (page < blocks_dev))
            def _():
                for copy in copies(device, block, page):
                    copy.start()
        return carry

    lax.fori_loop(0, seqs, scan, 0)
    pltpu.make_async_copy(k_cache, k_cache, sem.at[0]).wait()
    pltpu.make_async_copy(v_cache, v_cache, sem.at[1]).wait()


def body(seqs, tps, hidden, w_qkv, w_out, seg_ids, positions, page_table):
    rows, width = hidden.shape
    heads = width // HEAD_DIM
    chips = seqs // 2
    chip_bits = chips.bit_length() - 1
    chunks = len(row_sizes(rows))
    steps = rows // CHUNK
    blocks_dev = page_table.shape[0]
    long_rows = seqs * rows * 4 // 5
    half = HEAD_DIM // 2
    frequency = ROPE_BASE ** (-jnp.arange(half).astype(jnp.float32) * 2.0 / HEAD_DIM)
    angle = positions.astype(jnp.float32)[:, None] * frequency[None, :]
    cosine, sine = jnp.cos(angle), jnp.sin(angle)
    cos2 = jnp.concatenate([cosine, cosine], axis=1)
    sin2 = jnp.concatenate([-sine, sine], axis=1)
    seg_rows = rows // 128
    ints = jnp.concatenate([seg_ids, jnp.pad(page_table, (0, 3 * 128 - blocks_dev))]).reshape(seg_rows + 3, 128)
    anywhere = pl.BlockSpec(memory_space=pl.ANY)
    vmem = pl.BlockSpec(memory_space=pltpu.VMEM)
    kv_stage_copies = sum(2 << s for s in range(chip_bits)) + 1
    bf16, f32 = jnp.bfloat16, jnp.float32
    dma = pltpu.SemaphoreType.DMA
    delta, kv_all, ints_all = pl.pallas_call(
        functools.partial(sublayer_kernel, seqs, tps, long_rows),
        out_shape=(
            jax.ShapeDtypeStruct((rows, width), bf16),
            jax.ShapeDtypeStruct((2, chips, rows, 2 * width), bf16),
            jax.ShapeDtypeStruct((seqs, seg_rows + 3, 128), jnp.int32),
        ),
        in_specs=[anywhere, anywhere, anywhere, vmem, vmem, vmem],
        out_specs=(vmem, anywhere, vmem),
        scratch_shapes=[
            pltpu.VMEM(w_qkv.shape, bf16),
            pltpu.VMEM(w_out.shape, bf16),
            pltpu.VMEM((tps, rows, width), bf16),
            pltpu.VMEM((rows, width), bf16),
            pltpu.VMEM((2, chips, rows, 2 * width), bf16),
            pltpu.VMEM((heads, 1, rows), f32),
            pltpu.VMEM((heads, 1, rows), f32),
            pltpu.VMEM((heads, HEAD_DIM, rows), f32),
            pltpu.VMEM((width, rows), bf16),
            pltpu.VMEM((tps, rows, width), f32),
            pltpu.VMEM((tps, rows, width), bf16),
            pltpu.VMEM((tps, rows, width), bf16),
            pltpu.VMEM((tps, rows, width), bf16),
            dma((2, tps, chunks)), dma((2, tps, chunks)),
            dma((chunks, kv_stage_copies)), dma((chunks, kv_stage_copies)),
            dma((chip_bits + 1,)), dma((chip_bits + 1,)),
            dma((tps, steps)), dma((2, tps, steps)),
            dma((3,)), dma((chunks,)),
        ],
        compiler_params=pltpu.CompilerParams(
            collective_id=0, has_side_effects=True, vmem_limit_bytes=60 * 1024 * 1024),
    )(hidden, w_qkv, w_out, cos2, sin2, ints)
    k_cache, v_cache = pl.pallas_call(
        functools.partial(page_kernel, blocks_dev),
        out_shape=(jax.ShapeDtypeStruct((blocks_dev, PAGE, width), bf16),) * 2,
        in_specs=[pl.BlockSpec(memory_space=pltpu.SMEM), anywhere],
        out_specs=(anywhere, anywhere),
        scratch_shapes=[dma((2,))],
    )(ints_all, kv_all)
    return delta, k_cache, v_cache


def solution(mesh):
    in_specs = (P("seq", "tp"), P(None, None, "tp"), P("tp", None), P("seq"), P("seq"), P("seq"))
    out_specs = (P("seq", "tp"), P("seq", None, "tp"), P("seq", None, "tp"))
    return jax.shard_map(
        functools.partial(body, mesh.shape["seq"], mesh.shape["tp"]),
        mesh=mesh, in_specs=in_specs, out_specs=out_specs, check_vma=False)
```

```python
import functools
import math

import jax
import jax.numpy as jnp
import numpy as np
from jax import lax
from jax.sharding import PartitionSpec as P
from jax.experimental import pallas as pl
from jax.experimental.pallas import tpu as pltpu

HEAD_DIM = 128
PAGE = 16
ROPE_BASE = 10000.0
EPSILON = 1e-05
NEG_LARGE = -1e30
SCALE = HEAD_DIM ** -0.5 * math.log2(math.e)
MESH = pl.DeviceIdType.MESH
CHUNK = 128
STRADDLE = 128


def row_sizes(rows):
    return [64] + [128] * (rows // 128 - 1) + [64]


def flip(index, bit):
    return index + (1 << bit) * (1 - 2 * ((index // (1 << bit)) % 2))


def flips(index, bits):
    found = [index]
    for bit in bits:
        found = found + [flip(one, bit) for one in found]
    return found


def sublayer_kernel(seqs, tps, long_rows,
                    hid, wqkv, wout, frequency, segments, positions, table,
                    delta, k_cache, v_cache,
                    wq_s, wo_s, hfull, q_s, kv, m_s, l_s, acc_s, att_s, part, sendbuf, from_left, from_right,
                    ints_all, cos2, sin2, paged,
                    z_send, z_recv, kv_send, kv_recv, int_send, int_recv, rs_send, rs_recv, local_sem):
    me = lax.axis_index("seq")
    z = lax.axis_index("tp")
    core, chip = me % 2, me // 2
    chips = seqs // 2
    chip_bits = chips.bit_length() - 1
    rows_dev, width = hid.shape
    heads = width // HEAD_DIM
    sizes = row_sizes(rows_dev)
    offsets = [sum(sizes[:c]) for c in range(len(sizes))]
    chunks = len(sizes)
    steps = rows_dev // CHUNK
    split = long_rows % rows_dev

    barrier = pltpu.get_barrier_semaphore()
    for bit in range(chip_bits + 1):
        pl.semaphore_signal(barrier, inc=1, device_id={"seq": flip(me, bit)}, device_id_type=MESH)

    @pl.when(z > 0)
    def _():
        pl.semaphore_signal(barrier, inc=1, device_id={"tp": z - 1}, device_id_type=MESH)

    @pl.when(z < tps - 1)
    def _():
        pl.semaphore_signal(barrier, inc=1, device_id={"tp": z + 1}, device_id_type=MESH)

    load_h = pltpu.make_async_copy(hid, hfull.at[z], local_sem.at[0])
    load_q = pltpu.make_async_copy(wqkv, wq_s, local_sem.at[1])
    load_o = pltpu.make_async_copy(wout, wo_s, local_sem.at[2])
    load_h.start()
    load_q.start()
    load_o.start()
    neighbours = (z > 0).astype(jnp.int32) + (z < tps - 1).astype(jnp.int32)
    pl.semaphore_wait(barrier, chip_bits + 1 + neighbours)

    def chunk_rows(c):
        return pl.ds(offsets[c], sizes[c])

    def z_copy(way, hop, c):
        shard = z - way * (hop - 1)
        source = hid.at[chunk_rows(c)] if hop == 1 else hfull.at[shard, chunk_rows(c)]
        side = 0 if way > 0 else 1
        return pltpu.make_async_remote_copy(
            src_ref=source, dst_ref=hfull.at[shard, chunk_rows(c)],
            send_sem=z_send.at[side, hop, c], recv_sem=z_recv.at[side, hop, c],
            device_id={"tp": z + way}, device_id_type=MESH)

    def has(way, hop):
        ahead = z + 1 < tps if way > 0 else z > 0
        held = z - (hop - 1) >= 0 if way > 0 else z + (hop - 1) < tps
        return ahead & held

    def gets(way, hop):
        return z - hop >= 0 if way > 0 else z + hop < tps

    def z_start(way, hop, c):
        @pl.when(has(way, hop))
        def _():
            z_copy(way, hop, c).start()

    def z_arrive(way, hop, c):
        @pl.when(gets(way, hop))
        def _():
            z_copy(way, hop, c).wait_recv()

    def z_pass(hop, c):
        for way in (1, -1):
            z_arrive(way, hop, c)
            if hop + 1 < tps:
                z_start(way, hop + 1, c)

    orders = (list(range(chip_bits)), list(range(chip_bits))[::-1])
    def kv_copies(stage, c):
        found = []
        if stage == chip_bits:
            found.append((kv.at[core, :, chunk_rows(c)], {"seq": flip(me, 0)}))
        else:
            for side, order in enumerate(orders):
                half = sizes[c] // 2
                rows = pl.ds(offsets[c] + side * half, half)
                to = flip(chip, order[stage]) * 2 + core
                for shard in flips(chip, order[:stage]):
                    found.append((kv.at[core, shard, rows], {"seq": to}))
        base = sum(2 << s for s in range(stage))
        return [
            pltpu.make_async_remote_copy(
                src_ref=ref, dst_ref=ref, send_sem=kv_send.at[c, base + k], recv_sem=kv_recv.at[c, base + k],
                device_id=to, device_id_type=MESH)
            for k, (ref, to) in enumerate(found)
        ]

    def kv_start(stage, c):
        for copy in kv_copies(stage, c):
            copy.start()

    def kv_arrive(stage, c):
        for copy in kv_copies(stage, c):
            copy.wait_recv()

    for way in (1, -1):
        z_start(way, 1, 0)
    for way in (1, -1):
        z_start(way, 1, 1)

    lane_blocks = rows_dev // 128
    ints_all[me, :lane_blocks, :] = segments[...]
    pages = jnp.broadcast_to(table[...], (16, 128))
    pages = jnp.where(lax.broadcasted_iota(jnp.int32, (16, 128), 0) == 0, pages // 64, pages % 64)
    spread_out = jnp.where(
        lax.broadcasted_iota(jnp.int32, (128, rows_dev), 1) // PAGE == lax.broadcasted_iota(jnp.int32, (128, rows_dev), 0),
        1.0, 0.0)
    parts = jnp.dot(pages.astype(jnp.float32).astype(jnp.bfloat16), spread_out.astype(jnp.bfloat16),
                    preferred_element_type=jnp.float32).astype(jnp.int32)
    target_rows = (parts[0:1, :] * 64 + parts[1:2, :]) * PAGE + lax.broadcasted_iota(jnp.int32, (1, rows_dev), 1) % PAGE
    for block in range(lane_blocks):
        ints_all[me, lane_blocks + block:lane_blocks + block + 1, :] = target_rows[:, block * 128:(block + 1) * 128]

    def ints_copy(bit):
        first = (me // (1 << bit)) * (1 << bit)
        block = ints_all.at[pl.ds(first, 1 << bit)]
        return pltpu.make_async_remote_copy(
            src_ref=block, dst_ref=block, send_sem=int_send.at[bit], recv_sem=int_recv.at[bit],
            device_id={"seq": flip(me, bit)}, device_id_type=MESH)

    ints_copy(0).start()

    def down_columns(row):
        return jnp.transpose(jnp.broadcast_to(row.astype(jnp.float32), (128, 128)))

    turn = jnp.where(lax.broadcasted_iota(jnp.int32, (128, HEAD_DIM), 1) < HEAD_DIM // 2, -1.0, 1.0)
    for block in range(lane_blocks):
        angle = down_columns(positions[block:block + 1, :]) * frequency[...]
        cos2[block * 128:(block + 1) * 128, :] = jnp.cos(angle)
        sin2[block * 128:(block + 1) * 128, :] = jnp.sin(angle) * turn

    load_h.wait()
    load_q.wait()

    def project(c):
        rows = chunk_rows(c)
        pieces = [hfull[t, rows, :].astype(jnp.float32) for t in range(tps)]
        total = sum(jnp.sum(piece, axis=1, keepdims=True) for piece in pieces)
        mean = total * (1.0 / (tps * width))
        centred = [piece - mean for piece in pieces]
        spread = sum(jnp.sum(piece * piece, axis=1, keepdims=True) for piece in centred)
        factor = lax.rsqrt(spread * (1.0 / (tps * width)) + EPSILON)
        normed = jnp.concatenate([(piece * factor).astype(jnp.bfloat16) for piece in centred], axis=1)
        cos, sin = cos2[rows, :], sin2[rows, :]
        for which in range(3):
            projected = jnp.dot(normed, wq_s[which], preferred_element_type=jnp.float32)
            for h in range(heads):
                part_h = projected[:, h * HEAD_DIM:(h + 1) * HEAD_DIM]
                if which < 2:
                    part_h = part_h * cos + pltpu.roll(part_h, HEAD_DIM // 2, 1) * sin
                value = part_h.astype(jnp.bfloat16)
                if which == 0:
                    q_s[rows, h * HEAD_DIM:(h + 1) * HEAD_DIM] = value
                else:
                    at = (which - 1) * width + h * HEAD_DIM
                    kv[core, chip, rows, at:at + HEAD_DIM] = value

    def kv_next(stage, c):
        if 0 <= c < chunks:
            kv_arrive(stage, c)
            if stage < chip_bits:
                kv_start(stage + 1, c)

    for c in range(chunks):
        if c + 2 < chunks:
            for way in (1, -1):
                z_start(way, 1, c + 2)
        for hop in range(1, tps):
            z_pass(hop, c)
            if hop == 1:
                for stage in range(chip_bits - 1, 0, -1):
                    kv_next(stage, c - 1 - stage)
            if hop == 2:
                kv_next(0, c - 1)
        kv_next(chip_bits, c - chip_bits)
        if c <= chip_bits:
            ints_copy(c).wait()
            if c < chip_bits:
                ints_copy(c + 1).start()
        project(c)
        kv_start(0, c)
    if chunks <= chip_bits:
        for bit in range(chunks, chip_bits + 1):
            ints_copy(bit).wait()
            if bit < chip_bits:
                ints_copy(bit + 1).start()

    tiles = [(0, split), (split, rows_dev)] if split else [(0, rows_dev)]

    def seg_row(device):
        return [ints_all[device, r:r + 1, :] for r in range(lane_blocks)]

    def as_column(row):
        return down_columns(row)[:, :1]

    def score(key_at, h, tile):
        low, high = tile
        return lax.dot_general(kv[key_at + (pl.ds(h * HEAD_DIM, HEAD_DIM),)],
                               q_s[low:high, h * HEAD_DIM:(h + 1) * HEAD_DIM], (((1,), (1,)), ((), ())),
                               preferred_element_type=jnp.float32)

    def absorb(s, key_at, h, tile, mask, first):
        low, high = tile
        values = kv[key_at + (pl.ds(width + h * HEAD_DIM, HEAD_DIM),)]
        if mask is not None:
            s = jnp.where(mask, s, NEG_LARGE)
        top = jnp.max(s, axis=0, keepdims=True)
        if not first:
            before = m_s[h, :, low:high]
            top = jnp.maximum(top, before)
        p = jnp.exp2((s - top) * SCALE)
        total = jnp.sum(p, axis=0, keepdims=True)
        mixed = lax.dot_general(values, p.astype(jnp.bfloat16), (((0,), (0,)), ((), ())),
                                preferred_element_type=jnp.float32)
        if not first:
            alpha = jnp.exp2((before - top) * SCALE)
            total = total + alpha * l_s[h, :, low:high]
            mixed = mixed + alpha * acc_s[h, :, low:high]
        m_s[h, :, low:high] = top
        l_s[h, :, low:high] = total
        acc_s[h, :, low:high] = mixed

    def attend(units, mask=None, first=False):
        ahead = score(*units[0])
        for k, one in enumerate(units):
            now = ahead
            if k + 1 < len(units):
                ahead = score(*units[k + 1])
            absorb(now, *one, mask, first)

    own = seg_row(me)
    own_row = jnp.concatenate(own, axis=1).astype(jnp.float32)
    own_col = jnp.concatenate([as_column(row) for row in own], axis=0)
    starts_long = me * rows_dev < long_rows
    all_long = (me + 1) * rows_dev <= long_rows

    def attend_own(tile):
        low, high = tile
        key_index = lax.broadcasted_iota(jnp.int32, (high, high - low), 0)
        query_index = lax.broadcasted_iota(jnp.int32, (high, high - low), 1) + low
        mask = (own_col[:high] == own_row[:, low:high]) & (key_index <= query_index)
        attend([((core, chip, pl.ds(0, high)), h, tile) for h in range(heads)], mask, True)

    def attend_before(which, rows):
        tile = tiles[which]

        def attend_device(j, carry):
            attend([((j % 2, j // 2, rows), h, tile) for h in range(heads)])
            return carry

        lax.fori_loop(0, jnp.where(starts_long if which == 0 else all_long, me, 0), attend_device, 0)

    def attend_straddle():
        @pl.when(jnp.logical_not(starts_long))
        def _():
            before = me - 1
            row = ints_all[before, lane_blocks - 1:lane_blocks, :]
            low, high = tiles[0]
            mask = as_column(row) == own_row[:, low:high]
            at = (before % 2, before // 2, pl.ds(rows_dev - STRADDLE, STRADDLE))
            attend([(at, h, tiles[0]) for h in range(heads)], mask)

    def finish(tile):
        low, high = tile
        for h in range(heads):
            att_s[h * HEAD_DIM:(h + 1) * HEAD_DIM, low:high] = (
                acc_s[h, :, low:high] / l_s[h, :, low:high]).astype(jnp.bfloat16)

    def rs_copy(way, j, c):
        landing = from_left if way > 0 else from_right
        side = 0 if way > 0 else 1
        return pltpu.make_async_remote_copy(
            src_ref=sendbuf.at[j, step_rows(c)], dst_ref=landing.at[j, step_rows(c)],
            send_sem=rs_send.at[j, c], recv_sem=rs_recv.at[side, j, c],
            device_id={"tp": z + way}, device_id_type=MESH)

    ways = {1: list(range(tps - 1, 0, -1)), -1: list(range(0, tps - 1))}
    def step_rows(c):
        return pl.ds(c * CHUNK, CHUNK)

    def project_out(c):
        rows = step_rows(c)
        for j in range(tps):
            part[j, rows, :] = lax.dot_general(
                att_s[:, c * CHUNK:(c + 1) * CHUNK], wo_s[:, j * width:(j + 1) * width], (((0,), (0,)), ((), ())),
                preferred_element_type=jnp.float32)
        for way in (1, -1):
            @pl.when(z == (0 if way > 0 else tps - 1))
            def _():
                for j in ways[way]:
                    sendbuf[j, rows, :] = part[j, rows, :].astype(jnp.bfloat16)
                    rs_copy(way, j, c).start()

    last = chunks - 1
    early_rows = offsets[max(0, last - chip_bits + 1)]
    early, late = pl.ds(0, early_rows), pl.ds(early_rows, rows_dev - early_rows)
    work = [functools.partial(attend_own, tile) for tile in tiles]
    if early_rows:
        work += [functools.partial(attend_before, which, early) for which in range(len(tiles))]
    pending = [(c + min(stage + 1, chip_bits) + (stage == chip_bits) / 2, c, stage)
               for c in range(chunks) for stage in range(chip_bits + 1) if c + min(stage + 1, chip_bits) > last]
    pending = [(stage, c) for _, c, stage in sorted(pending)]
    places = (0, 1, len(pending) - 2, len(pending) - 1)
    for k, one in enumerate(pending):
        for place, task in zip(places, work):
            if place == k:
                task()
        kv_next(*one)
    load_o.wait()
    for which, tile in enumerate(tiles):
        attend_before(which, late)
        if which == 0:
            attend_straddle()
        finish(tile)
        for c in range(tile[0] // CHUNK, tile[1] // CHUNK):
            project_out(c)

    def place_from(device, carry):
        target = jnp.concatenate(
            [ints_all[device, lane_blocks + r:lane_blocks + r + 1, :] for r in range(lane_blocks)], axis=1)
        here = lax.broadcasted_iota(jnp.int32, (rows_dev, rows_dev), 0) + me * rows_dev
        pick = jnp.where(target == here, 1.0, 0.0).astype(jnp.bfloat16)
        paged[...] += jnp.dot(pick, kv[device % 2, device // 2], preferred_element_type=jnp.float32)
        return carry

    paged[...] = jnp.zeros(paged.shape, jnp.float32)
    for c in range(steps):
        rows = step_rows(c)
        lax.fori_loop(c * seqs // steps, (c + 1) * seqs // steps, place_from, 0)
        for hop in range(1, tps - 1):
            for way in (1, -1):
                landing = from_left if way > 0 else from_right

                @pl.when(z == (hop if way > 0 else tps - 1 - hop))
                def _():
                    for j in ways[way]:
                        if (j > hop) if way > 0 else (j < tps - 1 - hop):
                            rs_copy(way, j, c).wait_recv()
                            sendbuf[j, rows, :] = (
                                part[j, rows, :] + landing[j, rows, :].astype(jnp.float32)).astype(jnp.bfloat16)
                            rs_copy(way, j, c).start()

        @pl.when(z > 0)
        def _():
            rs_copy(1, z, c).wait_recv()
            part[z, rows, :] = part[z, rows, :] + from_left[z, rows, :].astype(jnp.float32)

        @pl.when(z < tps - 1)
        def _():
            rs_copy(-1, z, c).wait_recv()
            part[z, rows, :] = part[z, rows, :] + from_right[z, rows, :].astype(jnp.float32)

        delta[rows, :] = part[z, rows, :].astype(jnp.bfloat16)

    k_cache[...] = paged[:, :width].astype(jnp.bfloat16)
    v_cache[...] = paged[:, width:].astype(jnp.bfloat16)

    for c in range(chunks):
        for way in (1, -1):
            for hop in range(1, tps):
                @pl.when(has(way, hop))
                def _():
                    z_copy(way, hop, c).wait_send()
        for stage in range(chip_bits + 1):
            for copy in kv_copies(stage, c):
                copy.wait_send()
    for c in range(steps):
        for j in range(tps):
            @pl.when(z != j)
            def _():
                rs_copy(1, j, c).wait_send()


def body(seqs, tps, hidden, w_qkv, w_out, seg_ids, positions, page_table):
    rows, width = hidden.shape
    heads = width // HEAD_DIM
    chips = seqs // 2
    chip_bits = chips.bit_length() - 1
    chunks = len(row_sizes(rows))
    steps = rows // CHUNK
    blocks_dev = page_table.shape[0]
    long_rows = seqs * rows * 4 // 5
    half = HEAD_DIM // 2
    frequency = ROPE_BASE ** (-np.arange(half).astype(np.float64) * 2.0 / HEAD_DIM)
    frequency = jnp.asarray(np.concatenate([frequency, frequency])[None, :].astype(np.float32))
    lane_blocks = rows // 128
    assert blocks_dev <= 128
    anywhere = pl.BlockSpec(memory_space=pl.ANY)
    vmem = pl.BlockSpec(memory_space=pltpu.VMEM)
    kv_stage_copies = sum(2 << s for s in range(chip_bits)) + 1
    bf16, f32 = jnp.bfloat16, jnp.float32
    dma = pltpu.SemaphoreType.DMA
    delta, k_rows, v_rows = pl.pallas_call(
        functools.partial(sublayer_kernel, seqs, tps, long_rows),
        out_shape=(jax.ShapeDtypeStruct((rows, width), bf16),) * 3,
        in_specs=[anywhere, anywhere, anywhere, vmem, vmem, vmem, vmem],
        out_specs=(vmem, vmem, vmem),
        scratch_shapes=[
            pltpu.VMEM(w_qkv.shape, bf16),
            pltpu.VMEM(w_out.shape, bf16),
            pltpu.VMEM((tps, rows, width), bf16),
            pltpu.VMEM((rows, width), bf16),
            pltpu.VMEM((2, chips, rows, 2 * width), bf16),
            pltpu.VMEM((heads, 1, rows), f32),
            pltpu.VMEM((heads, 1, rows), f32),
            pltpu.VMEM((heads, HEAD_DIM, rows), f32),
            pltpu.VMEM((width, rows), bf16),
            pltpu.VMEM((tps, rows, width), f32),
            pltpu.VMEM((tps, rows, width), bf16),
            pltpu.VMEM((tps, rows, width), bf16),
            pltpu.VMEM((tps, rows, width), bf16),
            pltpu.VMEM((seqs, 2 * lane_blocks, 128), jnp.int32),
            pltpu.VMEM((rows, HEAD_DIM), f32),
            pltpu.VMEM((rows, HEAD_DIM), f32),
            pltpu.VMEM((rows, 2 * width), f32),
            dma((2, tps, chunks)), dma((2, tps, chunks)),
            dma((chunks, kv_stage_copies)), dma((chunks, kv_stage_copies)),
            dma((chip_bits + 1,)), dma((chip_bits + 1,)),
            dma((tps, steps)), dma((2, tps, steps)),
            dma((3,)),
        ],
        compiler_params=pltpu.CompilerParams(
            collective_id=0, has_side_effects=True, vmem_limit_bytes=60 * 1024 * 1024),
    )(hidden, w_qkv, w_out, frequency, seg_ids.reshape(lane_blocks, 128), positions.reshape(lane_blocks, 128),
      jnp.pad(page_table, (0, 128 - blocks_dev)).reshape(1, 128))
    return (delta, k_rows.reshape(blocks_dev, PAGE, width), v_rows.reshape(blocks_dev, PAGE, width))


def solution(mesh):
    in_specs = (P("seq", "tp"), P(None, None, "tp"), P("tp", None), P("seq"), P("seq"), P("seq"))
    out_specs = (P("seq", "tp"), P("seq", None, "tp"), P("seq", None, "tp"))
    return jax.shard_map(
        functools.partial(body, mesh.shape["seq"], mesh.shape["tp"]),
        mesh=mesh, in_specs=in_specs, out_specs=out_specs, check_vma=False)
```

```python
import functools
import math

import jax
import jax.numpy as jnp
import numpy as np
from jax import lax
from jax.sharding import PartitionSpec as P
from jax.experimental import pallas as pl
from jax.experimental.pallas import tpu as pltpu

HEAD_DIM = 128
PAGE = 16
ROPE_BASE = 10000.0
EPSILON = 1e-05
NEG_LARGE = -1e30
SCALE = HEAD_DIM ** -0.5 * math.log2(math.e)
MESH = pl.DeviceIdType.MESH
CHUNK = 128
STRADDLE = 128


def row_sizes(rows):
    return [64] + [128] * (rows // 128 - 1) + [64]


def flip(index, bit):
    return index + (1 << bit) * (1 - 2 * ((index // (1 << bit)) % 2))


def flips(index, bits):
    found = [index]
    for bit in bits:
        found = found + [flip(one, bit) for one in found]
    return found


def sublayer_kernel(seqs, tps, long_rows,
                    hid, wqkv, wout, frequency, segments, positions, table,
                    delta, k_cache, v_cache,
                    wq_s, wo_s, hfull, q_s, kv, m_s, l_s, acc_s, att_s, part, sendbuf, from_left, from_right,
                    ints_all, cos2, sin2, paged, sorted_rows, arrived, labels, labels_in,
                    z_send, z_recv, kv_send, kv_recv, int_send, int_recv, rs_send, rs_recv, page_send, page_recv, local_sem):
    me = lax.axis_index("seq")
    z = lax.axis_index("tp")
    core, chip = me % 2, me // 2
    chips = seqs // 2
    chip_bits = chips.bit_length() - 1
    rows_dev, width = hid.shape
    heads = width // HEAD_DIM
    sizes = row_sizes(rows_dev)
    offsets = [sum(sizes[:c]) for c in range(len(sizes))]
    chunks = len(sizes)
    steps = rows_dev // CHUNK
    split = long_rows % rows_dev

    barrier = pltpu.get_barrier_semaphore()
    for ahead in range(1, seqs):
        pl.semaphore_signal(barrier, inc=1, device_id={"seq": lax.rem(me + ahead, seqs)}, device_id_type=MESH)

    @pl.when(z > 0)
    def _():
        pl.semaphore_signal(barrier, inc=1, device_id={"tp": z - 1}, device_id_type=MESH)

    @pl.when(z < tps - 1)
    def _():
        pl.semaphore_signal(barrier, inc=1, device_id={"tp": z + 1}, device_id_type=MESH)

    load_h = pltpu.make_async_copy(hid, hfull.at[z], local_sem.at[0])
    load_q = pltpu.make_async_copy(wqkv, wq_s, local_sem.at[1])
    load_o = pltpu.make_async_copy(wout, wo_s, local_sem.at[2])
    load_h.start()
    load_q.start()
    load_o.start()
    neighbours = (z > 0).astype(jnp.int32) + (z < tps - 1).astype(jnp.int32)
    pl.semaphore_wait(barrier, seqs - 1 + neighbours)

    def chunk_rows(c):
        return pl.ds(offsets[c], sizes[c])

    def z_copy(way, hop, c):
        shard = z - way * (hop - 1)
        source = hid.at[chunk_rows(c)] if hop == 1 else hfull.at[shard, chunk_rows(c)]
        side = 0 if way > 0 else 1
        return pltpu.make_async_remote_copy(
            src_ref=source, dst_ref=hfull.at[shard, chunk_rows(c)],
            send_sem=z_send.at[side, hop, c], recv_sem=z_recv.at[side, hop, c],
            device_id={"tp": z + way}, device_id_type=MESH)

    def has(way, hop):
        ahead = z + 1 < tps if way > 0 else z > 0
        held = z - (hop - 1) >= 0 if way > 0 else z + (hop - 1) < tps
        return ahead & held

    def gets(way, hop):
        return z - hop >= 0 if way > 0 else z + hop < tps

    def z_start(way, hop, c):
        @pl.when(has(way, hop))
        def _():
            z_copy(way, hop, c).start()

    def z_arrive(way, hop, c):
        @pl.when(gets(way, hop))
        def _():
            z_copy(way, hop, c).wait_recv()

    def z_pass(hop, c):
        for way in (1, -1):
            z_arrive(way, hop, c)
            if hop + 1 < tps:
                z_start(way, hop + 1, c)

    capacity = -(-(rows_dev // PAGE) // seqs)
    used = capacity * PAGE
    ascending, descending = tuple(range(chip_bits)), tuple(range(chip_bits))[::-1]
    routes = ((0, ascending, 0), (0, descending, 1), (1, descending, None))

    def useful(shard, reached, rest, low_bit):
        farthest = reached
        for bit in rest:
            farthest = farthest + (1 << bit) * (1 - (reached // (1 << bit)) % 2)
        good = farthest > shard
        return good if low_bit is None else good & (shard % 2 == low_bit)

    def kv_copies(stage, c):
        found = []
        if stage == chip_bits:
            for k in range(chips):
                shard = lax.rem(chip + k, chips)
                needed = None if k == 0 else shard < chip
                found.append((k == 0, needed, needed, kv.at[core, shard, chunk_rows(c)], flip(me, 0)))
        else:
            for side, order, low_bit in routes:
                half = sizes[c] // 2
                rows = pl.ds(offsets[c] + side * half, half)
                partner = flip(chip, order[stage])
                mine, theirs = flips(chip, order[:stage]), flips(partner, order[:stage])
                for k, (shard, other) in enumerate(zip(mine, theirs)):
                    found.append((k == 0, useful(shard, partner, order[stage + 1:], low_bit),
                                  useful(other, chip, order[stage + 1:], low_bit),
                                  kv.at[core, shard, rows], partner * 2 + core))
        base = sum(len(routes) << s for s in range(stage))
        return [
            (own, sends, receives, pltpu.make_async_remote_copy(
                src_ref=ref, dst_ref=ref, send_sem=kv_send.at[c, base + k], recv_sem=kv_recv.at[c, base + k],
                device_id={"seq": to}, device_id_type=MESH))
            for k, (own, sends, receives, ref, to) in enumerate(found)
        ]

    def when(condition, act):
        if condition is None:
            act()
        else:
            pl.when(condition)(act)

    def kv_start(stage, c, own):
        for first, sends, _, copy in kv_copies(stage, c):
            if first == own:
                when(sends, copy.start)

    def kv_arrive(stage, c):
        for _, _, receives, copy in kv_copies(stage, c):
            when(receives, copy.wait_recv)

    for way in (1, -1):
        z_start(way, 1, 0)
    for way in (1, -1):
        z_start(way, 1, 1)

    lane_blocks = rows_dev // 128
    ints_all[me] = segments[...]

    def ints_copy(bit):
        first = (me // (1 << bit)) * (1 << bit)
        block = ints_all.at[pl.ds(first, 1 << bit)]
        return pltpu.make_async_remote_copy(
            src_ref=block, dst_ref=block, send_sem=int_send.at[bit], recv_sem=int_recv.at[bit],
            device_id={"seq": flip(me, bit)}, device_id_type=MESH)

    ints_copy(0).start()
    if used < 128:
        arrived[:, used:, :] = jnp.zeros((seqs, 128 - used, 2 * width), jnp.bfloat16)

    def down_columns(row):
        return jnp.transpose(jnp.broadcast_to(row.astype(jnp.float32), (128, 128)))

    turn = jnp.where(lax.broadcasted_iota(jnp.int32, (128, HEAD_DIM), 1) < HEAD_DIM // 2, -1.0, 1.0)
    for block in range(lane_blocks):
        angle = down_columns(positions[block:block + 1, :]) * frequency[...]
        cos2[block * 128:(block + 1) * 128, :] = jnp.cos(angle)
        sin2[block * 128:(block + 1) * 128, :] = jnp.sin(angle) * turn

    load_h.wait()
    load_q.wait()

    def project(c):
        rows = chunk_rows(c)
        pieces = [hfull[t, rows, :].astype(jnp.float32) for t in range(tps)]
        total = sum(jnp.sum(piece, axis=1, keepdims=True) for piece in pieces)
        mean = total * (1.0 / (tps * width))
        centred = [piece - mean for piece in pieces]
        spread = sum(jnp.sum(piece * piece, axis=1, keepdims=True) for piece in centred)
        factor = lax.rsqrt(spread * (1.0 / (tps * width)) + EPSILON)
        normed = jnp.concatenate([(piece * factor).astype(jnp.bfloat16) for piece in centred], axis=1)
        cos, sin = cos2[rows, :], sin2[rows, :]
        for which in range(3):
            projected = jnp.dot(normed, wq_s[which], preferred_element_type=jnp.float32)
            for h in range(heads):
                part_h = projected[:, h * HEAD_DIM:(h + 1) * HEAD_DIM]
                if which < 2:
                    part_h = part_h * cos + pltpu.roll(part_h, HEAD_DIM // 2, 1) * sin
                value = part_h.astype(jnp.bfloat16)
                if which == 0:
                    q_s[rows, h * HEAD_DIM:(h + 1) * HEAD_DIM] = value
                else:
                    at = (which - 1) * width + h * HEAD_DIM
                    kv[core, chip, rows, at:at + HEAD_DIM] = value

    def kv_next(stage, c):
        if 0 <= c < chunks:
            kv_arrive(stage, c)
            if stage < chip_bits:
                kv_start(stage + 1, c, False)

    for c in range(chunks):
        if c + 2 < chunks:
            for way in (1, -1):
                z_start(way, 1, c + 2)
        for hop in range(1, tps):
            z_pass(hop, c)
            if hop == 1:
                for stage in range(chip_bits - 1, 0, -1):
                    kv_next(stage, c - 1 - stage)
            if hop == 2:
                kv_next(0, c - 1)
        kv_next(chip_bits, c - chip_bits)
        if c <= chip_bits:
            ints_copy(c).wait()
            if c < chip_bits:
                ints_copy(c + 1).start()
        project(c)
        for stage in range(chip_bits + 1):
            kv_start(stage, c, True)
    if chunks <= chip_bits:
        for bit in range(chunks, chip_bits + 1):
            ints_copy(bit).wait()
            if bit < chip_bits:
                ints_copy(bit + 1).start()

    tiles = [(0, split), (split, rows_dev)] if split else [(0, rows_dev)]

    def seg_row(device):
        return [ints_all[device, r:r + 1, :] for r in range(lane_blocks)]

    def as_column(row):
        return down_columns(row)[:, :1]

    def score(key_at, h, tile):
        low, high = tile
        return lax.dot_general(kv[key_at + (pl.ds(h * HEAD_DIM, HEAD_DIM),)],
                               q_s[low:high, h * HEAD_DIM:(h + 1) * HEAD_DIM], (((1,), (1,)), ((), ())),
                               preferred_element_type=jnp.float32)

    def absorb(s, key_at, h, tile, mask, first):
        low, high = tile
        values = kv[key_at + (pl.ds(width + h * HEAD_DIM, HEAD_DIM),)]
        if mask is not None:
            s = jnp.where(mask, s, NEG_LARGE)
        top = jnp.max(s, axis=0, keepdims=True)
        if not first:
            before = m_s[h, :, low:high]
            top = jnp.maximum(top, before)
        p = jnp.exp2((s - top) * SCALE)
        total = jnp.sum(p, axis=0, keepdims=True)
        mixed = lax.dot_general(values, p.astype(jnp.bfloat16), (((0,), (0,)), ((), ())),
                                preferred_element_type=jnp.float32)
        if not first:
            alpha = jnp.exp2((before - top) * SCALE)
            total = total + alpha * l_s[h, :, low:high]
            mixed = mixed + alpha * acc_s[h, :, low:high]
        m_s[h, :, low:high] = top
        l_s[h, :, low:high] = total
        acc_s[h, :, low:high] = mixed

    def attend(units, mask=None, first=False):
        ahead = score(*units[0])
        for k, one in enumerate(units):
            now = ahead
            if k + 1 < len(units):
                ahead = score(*units[k + 1])
            absorb(now, *one, mask, first)

    own = seg_row(me)
    own_row = jnp.concatenate(own, axis=1).astype(jnp.float32)
    own_col = jnp.concatenate([as_column(row) for row in own], axis=0)
    starts_long = me * rows_dev < long_rows
    all_long = (me + 1) * rows_dev <= long_rows

    def attend_own(tile):
        low, high = tile
        key_index = lax.broadcasted_iota(jnp.int32, (high, high - low), 0)
        query_index = lax.broadcasted_iota(jnp.int32, (high, high - low), 1) + low
        mask = (own_col[:high] == own_row[:, low:high]) & (key_index <= query_index)
        attend([((core, chip, pl.ds(0, high)), h, tile) for h in range(heads)], mask, True)

    def attend_before(which, rows):
        tile = tiles[which]

        def attend_device(j, carry):
            attend([((j % 2, j // 2, rows), h, tile) for h in range(heads)])
            return carry

        lax.fori_loop(0, jnp.where(starts_long if which == 0 else all_long, me, 0), attend_device, 0)

    def attend_straddle():
        @pl.when(jnp.logical_not(starts_long))
        def _():
            before = me - 1
            row = ints_all[before, lane_blocks - 1:lane_blocks, :]
            low, high = tiles[0]
            mask = as_column(row) == own_row[:, low:high]
            at = (before % 2, before // 2, pl.ds(rows_dev - STRADDLE, STRADDLE))
            attend([(at, h, tiles[0]) for h in range(heads)], mask)

    def finish(tile):
        low, high = tile
        for h in range(heads):
            att_s[h * HEAD_DIM:(h + 1) * HEAD_DIM, low:high] = (
                acc_s[h, :, low:high] / l_s[h, :, low:high]).astype(jnp.bfloat16)

    def rs_copy(way, j, c):
        landing = from_left if way > 0 else from_right
        side = 0 if way > 0 else 1
        return pltpu.make_async_remote_copy(
            src_ref=sendbuf.at[j, step_rows(c)], dst_ref=landing.at[j, step_rows(c)],
            send_sem=rs_send.at[j, c], recv_sem=rs_recv.at[side, j, c],
            device_id={"tp": z + way}, device_id_type=MESH)

    ways = {1: list(range(tps - 1, 0, -1)), -1: list(range(0, tps - 1))}
    def step_rows(c):
        return pl.ds(c * CHUNK, CHUNK)

    def project_out(c):
        rows = step_rows(c)
        for j in range(tps):
            part[j, rows, :] = lax.dot_general(
                att_s[:, c * CHUNK:(c + 1) * CHUNK], wo_s[:, j * width:(j + 1) * width], (((0,), (0,)), ((), ())),
                preferred_element_type=jnp.float32)
        for way in (1, -1):
            @pl.when(z == (0 if way > 0 else tps - 1))
            def _():
                for j in ways[way]:
                    sendbuf[j, rows, :] = part[j, rows, :].astype(jnp.bfloat16)
                    rs_copy(way, j, c).start()

    last = chunks - 1
    early_rows = offsets[max(0, last - chip_bits + 1)]
    early, late = pl.ds(0, early_rows), pl.ds(early_rows, rows_dev - early_rows)
    work = [functools.partial(attend_own, tile) for tile in tiles]
    if early_rows:
        work += [functools.partial(attend_before, which, early) for which in range(len(tiles))]
    pending = [(c + min(stage + 1, chip_bits) + (stage == chip_bits) / 2, c, stage)
               for c in range(chunks) for stage in range(chip_bits + 1) if c + min(stage + 1, chip_bits) > last]
    pending = [(stage, c) for _, c, stage in sorted(pending)]
    places = (0, 1, len(pending) - 2, len(pending) - 1)
    for k, one in enumerate(pending):
        for place, task in zip(places, work):
            if place == k:
                task()
        kv_next(*one)
    load_o.wait()
    for which, tile in enumerate(tiles):
        attend_before(which, late)
        if which == 0:
            attend_straddle()
        finish(tile)
        for c in range(tile[0] // CHUNK, tile[1] // CHUNK):
            project_out(c)

    group = min(4, seqs)

    def page_copy(ahead, what):
        to, origin = lax.rem(me + ahead, seqs), me
        source, landing = (sorted_rows, arrived) if what == 0 else (labels, labels_in)
        if what == 0:
            source, landing = source.at[to, pl.ds(0, used)], landing.at[origin, pl.ds(0, used)]
        else:
            source, landing = source.at[to], landing.at[origin]
        return pltpu.make_async_remote_copy(
            src_ref=source, dst_ref=landing, send_sem=page_send.at[what, ahead], recv_sem=page_recv.at[what, ahead],
            device_id={"seq": to}, device_id_type=MESH)

    def send_pages():
        blocks = rows_dev // PAGE
        lane = lax.broadcasted_iota(jnp.int32, (128, 128), 1)
        sub = lax.broadcasted_iota(jnp.int32, (128, 128), 0)
        page = table[...].astype(jnp.float32)
        owner = jnp.where(lane[:1] < blocks, jnp.floor((page + 0.5) * (1.0 / blocks)), -1.0)
        same = (down_columns(owner) == owner) & (sub < lane)
        rank = jnp.sum(jnp.where(same, 1.0, 0.0), axis=0, keepdims=True)
        within = page - owner * blocks
        which = lax.broadcasted_iota(jnp.int32, (16, 128), 0)
        facts = jnp.where(which == 0, owner, jnp.where(which == 1, rank, within)).astype(jnp.bfloat16)
        row = lax.broadcasted_iota(jnp.int32, (128, rows_dev), 1)
        to_rows = jnp.where(row // PAGE == lax.broadcasted_iota(jnp.int32, (128, rows_dev), 0), 1.0, 0.0)
        facts = jnp.dot(facts, to_rows.astype(jnp.bfloat16), preferred_element_type=jnp.float32)
        in_page = (lax.broadcasted_iota(jnp.int32, (1, rows_dev), 1) % PAGE).astype(jnp.float32)
        slot = facts[0:1] * 128.0 + facts[1:2] * PAGE + in_page
        which = lax.broadcasted_iota(jnp.int32, (16, rows_dev), 0)
        marks = jnp.where(which == 0, facts[2:3] + 1.0, in_page).astype(jnp.bfloat16)
        mine = kv[core, chip]
        for first in range(0, seqs, group):
            here = lax.broadcasted_iota(jnp.int32, (group * 128, rows_dev), 0) + first * 128
            pick = jnp.where(slot == here.astype(jnp.float32), 1.0, 0.0).astype(jnp.bfloat16)
            rows = jnp.dot(pick, mine, preferred_element_type=jnp.float32).astype(jnp.bfloat16)
            sorted_rows[first:first + group] = rows.reshape(group, 128, 2 * width)
            marked = lax.dot_general(marks, pick, (((1,), (1,)), ((), ())), preferred_element_type=jnp.float32)
            label = jnp.where(marked[0:1] > 0.0, (marked[0:1] - 1.0) * PAGE + marked[1:2] + 1.0, 0.0).astype(jnp.int32)
            for k in range(group):
                labels[first + k] = label[:, k * 128:(k + 1) * 128]
        for ahead in range(1, seqs):
            for what in (0, 1):
                page_copy(ahead, what).start()

    def place_pages():
        for what in (0, 1):
            for ahead in range(1, seqs):
                page_copy(ahead, what).wait_recv()
        arrived[me, :used, :] = sorted_rows[me, :used, :]
        labels_in[me] = labels[me]
        paged[...] = jnp.zeros(paged.shape, jnp.float32)
        for first in range(0, seqs, group):
            label = jnp.concatenate([labels_in[first + k] for k in range(group)], axis=1)
            here = lax.broadcasted_iota(jnp.int32, (rows_dev, group * 128), 0) + 1
            pick = jnp.where(label == here, 1.0, 0.0).astype(jnp.bfloat16)
            rows = arrived[first:first + group].reshape(group * 128, 2 * width)
            paged[...] += jnp.dot(pick, rows, preferred_element_type=jnp.float32)

    send_pages()
    for c in range(steps):
        rows = step_rows(c)
        if c == steps - 2:
            place_pages()
        for hop in range(1, tps - 1):
            for way in (1, -1):
                landing = from_left if way > 0 else from_right

                @pl.when(z == (hop if way > 0 else tps - 1 - hop))
                def _():
                    for j in ways[way]:
                        if (j > hop) if way > 0 else (j < tps - 1 - hop):
                            rs_copy(way, j, c).wait_recv()
                            sendbuf[j, rows, :] = (
                                part[j, rows, :] + landing[j, rows, :].astype(jnp.float32)).astype(jnp.bfloat16)
                            rs_copy(way, j, c).start()

        @pl.when(z > 0)
        def _():
            rs_copy(1, z, c).wait_recv()
            part[z, rows, :] = part[z, rows, :] + from_left[z, rows, :].astype(jnp.float32)

        @pl.when(z < tps - 1)
        def _():
            rs_copy(-1, z, c).wait_recv()
            part[z, rows, :] = part[z, rows, :] + from_right[z, rows, :].astype(jnp.float32)

        delta[rows, :] = part[z, rows, :].astype(jnp.bfloat16)

    k_cache[...] = paged[:, :width].astype(jnp.bfloat16)
    v_cache[...] = paged[:, width:].astype(jnp.bfloat16)

    for ahead in range(1, seqs):
        for what in (0, 1):
            page_copy(ahead, what).wait_send()
    for c in range(chunks):
        for way in (1, -1):
            for hop in range(1, tps):
                @pl.when(has(way, hop))
                def _():
                    z_copy(way, hop, c).wait_send()
        for stage in range(chip_bits + 1):
            for _, sends, _, copy in kv_copies(stage, c):
                when(sends, copy.wait_send)
    for c in range(steps):
        for j in range(tps):
            @pl.when(z != j)
            def _():
                rs_copy(1, j, c).wait_send()


def body(seqs, tps, hidden, w_qkv, w_out, seg_ids, positions, page_table):
    rows, width = hidden.shape
    heads = width // HEAD_DIM
    chips = seqs // 2
    chip_bits = chips.bit_length() - 1
    chunks = len(row_sizes(rows))
    steps = rows // CHUNK
    blocks_dev = page_table.shape[0]
    long_rows = seqs * rows * 4 // 5
    half = HEAD_DIM // 2
    frequency = ROPE_BASE ** (-np.arange(half).astype(np.float64) * 2.0 / HEAD_DIM)
    frequency = jnp.asarray(np.concatenate([frequency, frequency])[None, :].astype(np.float32))
    lane_blocks = rows // 128
    assert blocks_dev <= 128
    anywhere = pl.BlockSpec(memory_space=pl.ANY)
    vmem = pl.BlockSpec(memory_space=pltpu.VMEM)
    kv_stage_copies = sum(3 << s for s in range(chip_bits)) + chips
    bf16, f32 = jnp.bfloat16, jnp.float32
    dma = pltpu.SemaphoreType.DMA
    delta, k_rows, v_rows = pl.pallas_call(
        functools.partial(sublayer_kernel, seqs, tps, long_rows),
        out_shape=(jax.ShapeDtypeStruct((rows, width), bf16),) * 3,
        in_specs=[anywhere, anywhere, anywhere, vmem, vmem, vmem, vmem],
        out_specs=(vmem, vmem, vmem),
        scratch_shapes=[
            pltpu.VMEM(w_qkv.shape, bf16),
            pltpu.VMEM(w_out.shape, bf16),
            pltpu.VMEM((tps, rows, width), bf16),
            pltpu.VMEM((rows, width), bf16),
            pltpu.VMEM((2, chips, rows, 2 * width), bf16),
            pltpu.VMEM((heads, 1, rows), f32),
            pltpu.VMEM((heads, 1, rows), f32),
            pltpu.VMEM((heads, HEAD_DIM, rows), f32),
            pltpu.VMEM((width, rows), bf16),
            pltpu.VMEM((tps, rows, width), f32),
            pltpu.VMEM((tps, rows, width), bf16),
            pltpu.VMEM((tps, rows, width), bf16),
            pltpu.VMEM((tps, rows, width), bf16),
            pltpu.VMEM((seqs, lane_blocks, 128), jnp.int32),
            pltpu.VMEM((rows, HEAD_DIM), f32),
            pltpu.VMEM((rows, HEAD_DIM), f32),
            pltpu.VMEM((rows, 2 * width), f32),
            pltpu.VMEM((seqs, 128, 2 * width), bf16),
            pltpu.VMEM((seqs, 128, 2 * width), bf16),
            pltpu.VMEM((seqs, 1, 128), jnp.int32),
            pltpu.VMEM((seqs, 1, 128), jnp.int32),
            dma((2, tps, chunks)), dma((2, tps, chunks)),
            dma((chunks, kv_stage_copies)), dma((chunks, kv_stage_copies)),
            dma((chip_bits + 1,)), dma((chip_bits + 1,)),
            dma((tps, steps)), dma((2, tps, steps)),
            dma((2, seqs)), dma((2, seqs)),
            dma((3,)),
        ],
        compiler_params=pltpu.CompilerParams(
            collective_id=0, has_side_effects=True, vmem_limit_bytes=60 * 1024 * 1024),
    )(hidden, w_qkv, w_out, frequency, seg_ids.reshape(lane_blocks, 128), positions.reshape(lane_blocks, 128),
      jnp.pad(page_table, (0, 128 - blocks_dev)).reshape(1, 128))
    return (delta, k_rows.reshape(blocks_dev, PAGE, width), v_rows.reshape(blocks_dev, PAGE, width))


def solution(mesh):
    in_specs = (P("seq", "tp"), P(None, None, "tp"), P("tp", None), P("seq"), P("seq"), P("seq"))
    out_specs = (P("seq", "tp"), P("seq", None, "tp"), P("seq", None, "tp"))
    return jax.shard_map(
        functools.partial(body, mesh.shape["seq"], mesh.shape["tp"]),
        mesh=mesh, in_specs=in_specs, out_specs=out_specs, check_vma=False)
```

```python
import functools
import math

import jax
import jax.numpy as jnp
import numpy as np
from jax import lax
from jax.sharding import PartitionSpec as P
from jax.experimental import pallas as pl
from jax.experimental.pallas import tpu as pltpu

HEAD_DIM = 128
PAGE = 16
ROPE_BASE = 10000.0
EPSILON = 1e-05
NEG_LARGE = -1e30
SCALE = HEAD_DIM ** -0.5 * math.log2(math.e)
MESH = pl.DeviceIdType.MESH
CHUNK = 128
STRADDLE = 128


def row_sizes(rows):
    return [64] + [128] * (rows // 128 - 1) + [64]


def flip(index, bit):
    return index + (1 << bit) * (1 - 2 * ((index // (1 << bit)) % 2))


def flips(index, bits):
    found = [index]
    for bit in bits:
        found = found + [flip(one, bit) for one in found]
    return found


def sublayer_kernel(seqs, tps, long_rows,
                    hid, wqkv, wout, frequency, segments, positions, table,
                    delta, k_cache, v_cache,
                    wq_s, wo_s, hfull, q_s, kv, m_s, l_s, acc_s, att_s, part, sendbuf, from_left, from_right,
                    ints_all, cos2, sin2, paged, wo_end, att_end, sorted_rows, arrived, labels, labels_in,
                    z_send, z_recv, kv_send, kv_recv, int_send, int_recv, rs_send, rs_recv, page_send, page_recv, end_send, end_recv, local_sem):
    me = lax.axis_index("seq")
    z = lax.axis_index("tp")
    core, chip = me % 2, me // 2
    chips = seqs // 2
    chip_bits = chips.bit_length() - 1
    rows_dev, width = hid.shape
    heads = width // HEAD_DIM
    sizes = row_sizes(rows_dev)
    offsets = [sum(sizes[:c]) for c in range(len(sizes))]
    chunks = len(sizes)
    steps = rows_dev // CHUNK
    split = long_rows % rows_dev

    barrier = pltpu.get_barrier_semaphore()
    for ahead in range(1, seqs):
        pl.semaphore_signal(barrier, inc=1, device_id={"seq": lax.rem(me + ahead, seqs)}, device_id_type=MESH)

    @pl.when(z > 0)
    def _():
        pl.semaphore_signal(barrier, inc=1, device_id={"tp": z - 1}, device_id_type=MESH)

    @pl.when(z < tps - 1)
    def _():
        pl.semaphore_signal(barrier, inc=1, device_id={"tp": z + 1}, device_id_type=MESH)

    load_h = pltpu.make_async_copy(hid, hfull.at[z], local_sem.at[0])
    load_q = pltpu.make_async_copy(wqkv, wq_s, local_sem.at[1])
    load_o = pltpu.make_async_copy(wout, wo_s, local_sem.at[2])
    load_h.start()
    load_q.start()
    load_o.start()
    neighbours = (z > 0).astype(jnp.int32) + (z < tps - 1).astype(jnp.int32)
    pl.semaphore_wait(barrier, seqs - 1 + neighbours)

    def chunk_rows(c):
        return pl.ds(offsets[c], sizes[c])

    def z_copy(way, hop, c):
        shard = z - way * (hop - 1)
        source = hid.at[chunk_rows(c)] if hop == 1 else hfull.at[shard, chunk_rows(c)]
        side = 0 if way > 0 else 1
        return pltpu.make_async_remote_copy(
            src_ref=source, dst_ref=hfull.at[shard, chunk_rows(c)],
            send_sem=z_send.at[side, hop, c], recv_sem=z_recv.at[side, hop, c],
            device_id={"tp": z + way}, device_id_type=MESH)

    def has(way, hop):
        ahead = z + 1 < tps if way > 0 else z > 0
        held = z - (hop - 1) >= 0 if way > 0 else z + (hop - 1) < tps
        return ahead & held

    def gets(way, hop):
        return z - hop >= 0 if way > 0 else z + hop < tps

    def z_start(way, hop, c):
        @pl.when(has(way, hop))
        def _():
            z_copy(way, hop, c).start()

    def z_arrive(way, hop, c):
        @pl.when(gets(way, hop))
        def _():
            z_copy(way, hop, c).wait_recv()

    def z_pass(hop, c):
        for way in (1, -1):
            z_arrive(way, hop, c)
            if hop + 1 < tps:
                z_start(way, hop + 1, c)

    capacity = -(-(rows_dev // PAGE) // seqs)
    used = capacity * PAGE
    ascending, descending = tuple(range(chip_bits)), tuple(range(chip_bits))[::-1]
    routes = ((0, ascending, 0), (0, descending, 1), (1, descending, None))

    def useful(shard, reached, rest, low_bit):
        farthest = reached
        for bit in rest:
            farthest = farthest + (1 << bit) * (1 - (reached // (1 << bit)) % 2)
        good = farthest > shard
        return good if low_bit is None else good & (shard % 2 == low_bit)

    def kv_copies(stage, c):
        found = []
        if stage == chip_bits:
            for k in range(chips):
                shard = lax.rem(chip + k, chips)
                needed = None if k == 0 else shard < chip
                found.append((k == 0, needed, needed, kv.at[core, shard, chunk_rows(c)], flip(me, 0)))
        else:
            for side, order, low_bit in routes:
                half = sizes[c] // 2
                rows = pl.ds(offsets[c] + side * half, half)
                partner = flip(chip, order[stage])
                mine, theirs = flips(chip, order[:stage]), flips(partner, order[:stage])
                for k, (shard, other) in enumerate(zip(mine, theirs)):
                    found.append((k == 0, useful(shard, partner, order[stage + 1:], low_bit),
                                  useful(other, chip, order[stage + 1:], low_bit),
                                  kv.at[core, shard, rows], partner * 2 + core))
        base = sum(len(routes) << s for s in range(stage))
        return [
            (own, sends, receives, pltpu.make_async_remote_copy(
                src_ref=ref, dst_ref=ref, send_sem=kv_send.at[c, base + k], recv_sem=kv_recv.at[c, base + k],
                device_id={"seq": to}, device_id_type=MESH))
            for k, (own, sends, receives, ref, to) in enumerate(found)
        ]

    def when(condition, act):
        if condition is None:
            act()
        else:
            pl.when(condition)(act)

    def kv_start(stage, c, own):
        for first, sends, _, copy in kv_copies(stage, c):
            if first == own:
                when(sends, copy.start)

    def kv_arrive(stage, c):
        for _, _, receives, copy in kv_copies(stage, c):
            when(receives, copy.wait_recv)

    for way in (1, -1):
        z_start(way, 1, 0)
    for way in (1, -1):
        z_start(way, 1, 1)

    lane_blocks = rows_dev // 128
    ints_all[me] = segments[...]

    def ints_copy(bit):
        first = (me // (1 << bit)) * (1 << bit)
        block = ints_all.at[pl.ds(first, 1 << bit)]
        return pltpu.make_async_remote_copy(
            src_ref=block, dst_ref=block, send_sem=int_send.at[bit], recv_sem=int_recv.at[bit],
            device_id={"seq": flip(me, bit)}, device_id_type=MESH)

    ints_copy(0).start()
    if used < 128:
        arrived[:, used:, :] = jnp.zeros((seqs, 128 - used, 2 * width), jnp.bfloat16)

    def down_columns(row):
        return jnp.transpose(jnp.broadcast_to(row.astype(jnp.float32), (128, 128)))

    turn = jnp.where(lax.broadcasted_iota(jnp.int32, (128, HEAD_DIM), 1) < HEAD_DIM // 2, -1.0, 1.0)
    for block in range(lane_blocks):
        angle = down_columns(positions[block:block + 1, :]) * frequency[...]
        cos2[block * 128:(block + 1) * 128, :] = jnp.cos(angle)
        sin2[block * 128:(block + 1) * 128, :] = jnp.sin(angle) * turn

    load_h.wait()
    load_q.wait()

    def project(c):
        rows = chunk_rows(c)
        pieces = [hfull[t, rows, :].astype(jnp.float32) for t in range(tps)]
        total = sum(jnp.sum(piece, axis=1, keepdims=True) for piece in pieces)
        mean = total * (1.0 / (tps * width))
        centred = [piece - mean for piece in pieces]
        spread = sum(jnp.sum(piece * piece, axis=1, keepdims=True) for piece in centred)
        factor = lax.rsqrt(spread * (1.0 / (tps * width)) + EPSILON)
        normed = jnp.concatenate([(piece * factor).astype(jnp.bfloat16) for piece in centred], axis=1)
        cos, sin = cos2[rows, :], sin2[rows, :]
        for which in range(3):
            projected = jnp.dot(normed, wq_s[which], preferred_element_type=jnp.float32)
            for h in range(heads):
                part_h = projected[:, h * HEAD_DIM:(h + 1) * HEAD_DIM]
                if which < 2:
                    part_h = part_h * cos + pltpu.roll(part_h, HEAD_DIM // 2, 1) * sin
                value = part_h.astype(jnp.bfloat16)
                if which == 0:
                    q_s[rows, h * HEAD_DIM:(h + 1) * HEAD_DIM] = value
                else:
                    at = (which - 1) * width + h * HEAD_DIM
                    kv[core, chip, rows, at:at + HEAD_DIM] = value

    def kv_next(stage, c):
        if 0 <= c < chunks:
            kv_arrive(stage, c)
            if stage < chip_bits:
                kv_start(stage + 1, c, False)

    is_end = (z == 0) | (z == tps - 1)
    is_helper = (z == 1) | (z == tps - 2)
    beside = jnp.where(z == 0, 1, tps - 2)
    half_rows = pl.ds(core * (width // 2), width // 2)
    pieces = 4

    def weights_copy(piece):
        size = width // 2 // pieces
        at = pl.ds(core * (width // 2) + piece * size, size)
        return pltpu.make_async_remote_copy(
            src_ref=wout.at[at], dst_ref=wo_end.at[at], send_sem=end_send.at[3 + piece], recv_sem=end_recv.at[3 + piece],
            device_id={"tp": beside}, device_id_type=MESH)

    weights_share = pltpu.make_async_remote_copy(
        src_ref=wo_end.at[half_rows], dst_ref=wo_end.at[half_rows], send_sem=end_send.at[2], recv_sem=end_recv.at[2],
        device_id={"seq": flip(me, 0)}, device_id_type=MESH)

    for c in range(chunks):
        if c + 2 < chunks:
            for way in (1, -1):
                z_start(way, 1, c + 2)
        for piece in range(c * pieces // (chunks - 2), min((c + 1) * pieces // (chunks - 2), pieces)):
            pl.when(is_end)(weights_copy(piece).start)
        for hop in range(1, tps):
            z_pass(hop, c)
        if c <= chip_bits:
            ints_copy(c).wait()
            if c < chip_bits:
                ints_copy(c + 1).start()
        project(c)
        for stage in range(chip_bits + 1):
            kv_start(stage, c, True)
        kv_next(0, c - 1)
        for stage in range(1, chip_bits):
            kv_next(stage, c - 1 - stage)
        kv_next(chip_bits, c - chip_bits)

    if chunks <= chip_bits:
        for bit in range(chunks, chip_bits + 1):
            ints_copy(bit).wait()
            if bit < chip_bits:
                ints_copy(bit + 1).start()

    tiles = [(0, split), (split, rows_dev)] if split else [(0, rows_dev)]

    def seg_row(device):
        return [ints_all[device, r:r + 1, :] for r in range(lane_blocks)]

    def as_column(row):
        return down_columns(row)[:, :1]

    def score(key_at, h, tile):
        low, high = tile
        return lax.dot_general(kv[key_at + (pl.ds(h * HEAD_DIM, HEAD_DIM),)],
                               q_s[low:high, h * HEAD_DIM:(h + 1) * HEAD_DIM], (((1,), (1,)), ((), ())),
                               preferred_element_type=jnp.float32)

    def absorb(s, key_at, h, tile, mask, first):
        low, high = tile
        values = kv[key_at + (pl.ds(width + h * HEAD_DIM, HEAD_DIM),)]
        if mask is not None:
            s = jnp.where(mask, s, NEG_LARGE)
        top = jnp.max(s, axis=0, keepdims=True)
        if not first:
            before = m_s[h, :, low:high]
            top = jnp.maximum(top, before)
        p = jnp.exp2((s - top) * SCALE)
        total = jnp.sum(p, axis=0, keepdims=True)
        mixed = lax.dot_general(values, p.astype(jnp.bfloat16), (((0,), (0,)), ((), ())),
                                preferred_element_type=jnp.float32)
        if not first:
            alpha = jnp.exp2((before - top) * SCALE)
            total = total + alpha * l_s[h, :, low:high]
            mixed = mixed + alpha * acc_s[h, :, low:high]
        m_s[h, :, low:high] = top
        l_s[h, :, low:high] = total
        acc_s[h, :, low:high] = mixed

    def attend(units, mask=None, first=False):
        ahead = score(*units[0])
        for k, one in enumerate(units):
            now = ahead
            if k + 1 < len(units):
                ahead = score(*units[k + 1])
            absorb(now, *one, mask, first)

    own = seg_row(me)
    own_row = jnp.concatenate(own, axis=1).astype(jnp.float32)
    own_col = jnp.concatenate([as_column(row) for row in own], axis=0)
    starts_long = me * rows_dev < long_rows
    all_long = (me + 1) * rows_dev <= long_rows

    def attend_own(tile):
        low, high = tile
        key_index = lax.broadcasted_iota(jnp.int32, (high, high - low), 0)
        query_index = lax.broadcasted_iota(jnp.int32, (high, high - low), 1) + low
        mask = (own_col[:high] == own_row[:, low:high]) & (key_index <= query_index)
        attend([((core, chip, pl.ds(0, high)), h, tile) for h in range(heads)], mask, True)

    def attend_before(which, rows):
        tile = tiles[which]

        def attend_device(j, carry):
            attend([((j % 2, j // 2, rows), h, tile) for h in range(heads)])
            return carry

        lax.fori_loop(0, jnp.where(starts_long if which == 0 else all_long, me, 0), attend_device, 0)

    def attend_straddle():
        @pl.when(jnp.logical_not(starts_long))
        def _():
            before = me - 1
            row = ints_all[before, lane_blocks - 1:lane_blocks, :]
            low, high = tiles[0]
            mask = as_column(row) == own_row[:, low:high]
            at = (before % 2, before // 2, pl.ds(rows_dev - STRADDLE, STRADDLE))
            attend([(at, h, tiles[0]) for h in range(heads)], mask)

    def finish(tile):
        low, high = tile
        for h in range(heads):
            att_s[h * HEAD_DIM:(h + 1) * HEAD_DIM, low:high] = (
                acc_s[h, :, low:high] / l_s[h, :, low:high]).astype(jnp.bfloat16)

    def rs_copy(way, j, c):
        landing = from_left if way > 0 else from_right
        side = 0 if way > 0 else 1
        return pltpu.make_async_remote_copy(
            src_ref=sendbuf.at[j, step_rows(c)], dst_ref=landing.at[j, step_rows(c)],
            send_sem=rs_send.at[j, c], recv_sem=rs_recv.at[side, j, c],
            device_id={"tp": z + way}, device_id_type=MESH)

    ways = {1: list(range(tps - 1, 0, -1)), -1: list(range(0, tps - 1))}
    def step_rows(c):
        return pl.ds(c * CHUNK, CHUNK)

    def end_copy(which):
        low, high = tiles[which]
        there = att_end.at[:, low:high]
        return pltpu.make_async_remote_copy(
            src_ref=att_s.at[:, low:high], dst_ref=there, send_sem=end_send.at[which], recv_sem=end_recv.at[which],
            device_id={"tp": beside}, device_id_type=MESH)

    def project_out(tile):
        low, high = tile
        rows = pl.ds(low, high - low)

        def times(attended, weights, j):
            return lax.dot_general(
                attended[:, low:high], weights[:, j * width:(j + 1) * width], (((0,), (0,)), ((), ())),
                preferred_element_type=jnp.float32)

        @pl.when(is_helper)
        def _():
            for j in range(tps):
                part[j, rows, :] = times(att_s, wo_s, j) + times(att_end, wo_end, j)

        @pl.when(jnp.logical_not(is_helper | is_end))
        def _():
            for j in range(tps):
                part[j, rows, :] = times(att_s, wo_s, j)

        for way in (1, -1):
            @pl.when(z == (1 if way > 0 else tps - 2))
            def _():
                for j in ways[way]:
                    if (j > 1) if way > 0 else (j < tps - 2):
                        sendbuf[j, rows, :] = part[j, rows, :].astype(jnp.bfloat16)
                for c in range(low // CHUNK, high // CHUNK):
                    for j in ways[way]:
                        if (j > 1) if way > 0 else (j < tps - 2):
                            rs_copy(way, j, c).start()

    group = min(4, seqs)

    def page_copy(ahead, what):
        to, origin = lax.rem(me + ahead, seqs), me
        source, landing = (sorted_rows, arrived) if what == 0 else (labels, labels_in)
        if what == 0:
            source, landing = source.at[to, pl.ds(0, used)], landing.at[origin, pl.ds(0, used)]
        else:
            source, landing = source.at[to], landing.at[origin]
        return pltpu.make_async_remote_copy(
            src_ref=source, dst_ref=landing, send_sem=page_send.at[what, ahead], recv_sem=page_recv.at[what, ahead],
            device_id={"seq": to}, device_id_type=MESH)

    def sort_pages():
        blocks = rows_dev // PAGE
        lane = lax.broadcasted_iota(jnp.int32, (128, 128), 1)
        sub = lax.broadcasted_iota(jnp.int32, (128, 128), 0)
        page = table[...].astype(jnp.float32)
        owner = jnp.where(lane[:1] < blocks, jnp.floor((page + 0.5) * (1.0 / blocks)), -1.0)
        same = (down_columns(owner) == owner) & (sub < lane)
        rank = jnp.sum(jnp.where(same, 1.0, 0.0), axis=0, keepdims=True)
        within = page - owner * blocks
        which = lax.broadcasted_iota(jnp.int32, (16, 128), 0)
        facts = jnp.where(which == 0, owner, jnp.where(which == 1, rank, within)).astype(jnp.bfloat16)
        row = lax.broadcasted_iota(jnp.int32, (128, rows_dev), 1)
        to_rows = jnp.where(row // PAGE == lax.broadcasted_iota(jnp.int32, (128, rows_dev), 0), 1.0, 0.0)
        facts = jnp.dot(facts, to_rows.astype(jnp.bfloat16), preferred_element_type=jnp.float32)
        in_page = (lax.broadcasted_iota(jnp.int32, (1, rows_dev), 1) % PAGE).astype(jnp.float32)
        slot = facts[0:1] * 128.0 + facts[1:2] * PAGE + in_page
        which = lax.broadcasted_iota(jnp.int32, (16, rows_dev), 0)
        marks = jnp.where(which == 0, facts[2:3] + 1.0, in_page).astype(jnp.bfloat16)
        mine = kv[core, chip]
        for first in range(0, seqs, group):
            here = lax.broadcasted_iota(jnp.int32, (group * 128, rows_dev), 0) + first * 128
            pick = jnp.where(slot == here.astype(jnp.float32), 1.0, 0.0).astype(jnp.bfloat16)
            rows = jnp.dot(pick, mine, preferred_element_type=jnp.float32).astype(jnp.bfloat16)
            sorted_rows[first:first + group] = rows.reshape(group, 128, 2 * width)
            marked = lax.dot_general(marks, pick, (((1,), (1,)), ((), ())), preferred_element_type=jnp.float32)
            label = jnp.where(marked[0:1] > 0.0, (marked[0:1] - 1.0) * PAGE + marked[1:2] + 1.0, 0.0).astype(jnp.int32)
            for k in range(group):
                labels[first + k] = label[:, k * 128:(k + 1) * 128]

    def place_pages():
        for what in (0, 1):
            for ahead in range(1, seqs):
                page_copy(ahead, what).wait_recv()
        arrived[me, :used, :] = sorted_rows[me, :used, :]
        labels_in[me] = labels[me]
        paged[...] = jnp.zeros(paged.shape, jnp.float32)
        for first in range(0, seqs, group):
            label = jnp.concatenate([labels_in[first + k] for k in range(group)], axis=1)
            here = lax.broadcasted_iota(jnp.int32, (rows_dev, group * 128), 0) + 1
            pick = jnp.where(label == here, 1.0, 0.0).astype(jnp.bfloat16)
            rows = arrived[first:first + group].reshape(group * 128, 2 * width)
            paged[...] += jnp.dot(pick, rows, preferred_element_type=jnp.float32)

    last = chunks - 1
    early_rows = offsets[max(0, last - chip_bits + 1)]
    early, late = pl.ds(0, early_rows), pl.ds(early_rows, rows_dev - early_rows)
    work = [sort_pages, lambda: [attend_own(tile) for tile in tiles]]
    if early_rows:
        work += [functools.partial(attend_before, which, early) for which in range(len(tiles))]
    pending = [(c + min(stage + 1, chip_bits) + (stage == chip_bits) / 2, c, stage)
               for c in range(chunks) for stage in range(chip_bits + 1) if c + min(stage + 1, chip_bits) > last]
    pending = [(stage, c) for _, stage, c in sorted((slot, stage, c) for slot, c, stage in pending)]
    places = (0, 1, len(pending) - 2, len(pending) - 1)
    for k, one in enumerate(pending):
        for place, task in zip(places, work):
            if place == k:
                task()
        kv_next(*one)
    for ahead in range(1, seqs):
        for what in (0, 1):
            page_copy(ahead, what).start()
    load_o.wait()

    @pl.when(is_helper)
    def _():
        for piece in range(pieces):
            weights_copy(piece).wait_recv()
        weights_share.start()

    for which, tile in enumerate(tiles):
        attend_before(which, late)
        if which == 0:
            attend_straddle()
        finish(tile)
        pl.when(is_end)(end_copy(which).start)

    @pl.when(is_helper)
    def _():
        weights_share.wait()

    for which, tile in enumerate(tiles):
        pl.when(is_helper)(end_copy(which).wait_recv)
        project_out(tile)

    for c in range(steps):
        rows = step_rows(c)
        for hop in range(2, tps - 1):
            for way in (1, -1):
                landing = from_left if way > 0 else from_right

                @pl.when(z == (hop if way > 0 else tps - 1 - hop))
                def _():
                    for j in ways[way]:
                        if (j > hop) if way > 0 else (j < tps - 1 - hop):
                            rs_copy(way, j, c).wait_recv()
                            sendbuf[j, rows, :] = (
                                part[j, rows, :] + landing[j, rows, :].astype(jnp.float32)).astype(jnp.bfloat16)
                            rs_copy(way, j, c).start()

        if c == steps - 1:
            place_pages()

        @pl.when(z == 0)
        def _():
            rs_copy(-1, 0, c).wait_recv()
            delta[rows, :] = from_right[0, rows, :]

        @pl.when(z == tps - 1)
        def _():
            rs_copy(1, tps - 1, c).wait_recv()
            delta[rows, :] = from_left[tps - 1, rows, :]

        @pl.when((z > 1) & (z < tps - 1))
        def _():
            rs_copy(1, z, c).wait_recv()
            part[z, rows, :] = part[z, rows, :] + from_left[z, rows, :].astype(jnp.float32)

        @pl.when((z > 0) & (z < tps - 2))
        def _():
            rs_copy(-1, z, c).wait_recv()
            part[z, rows, :] = part[z, rows, :] + from_right[z, rows, :].astype(jnp.float32)

        @pl.when(jnp.logical_not(is_end))
        def _():
            delta[rows, :] = part[z, rows, :].astype(jnp.bfloat16)

    k_cache[...] = paged[:, :width].astype(jnp.bfloat16)
    v_cache[...] = paged[:, width:].astype(jnp.bfloat16)

    for piece in range(pieces):
        pl.when(is_end)(weights_copy(piece).wait_send)
    for which in range(len(tiles)):
        pl.when(is_end)(end_copy(which).wait_send)
    for ahead in range(1, seqs):
        for what in (0, 1):
            page_copy(ahead, what).wait_send()
    for c in range(chunks):
        for way in (1, -1):
            for hop in range(1, tps):
                @pl.when(has(way, hop))
                def _():
                    z_copy(way, hop, c).wait_send()
        for stage in range(chip_bits + 1):
            for _, sends, _, copy in kv_copies(stage, c):
                when(sends, copy.wait_send)
    for c in range(steps):
        for j in range(tps):
            @pl.when((z != j) & jnp.logical_not(is_end))
            def _():
                rs_copy(1, j, c).wait_send()


def body(seqs, tps, hidden, w_qkv, w_out, seg_ids, positions, page_table):
    rows, width = hidden.shape
    heads = width // HEAD_DIM
    chips = seqs // 2
    chip_bits = chips.bit_length() - 1
    chunks = len(row_sizes(rows))
    steps = rows // CHUNK
    blocks_dev = page_table.shape[0]
    long_rows = seqs * rows * 4 // 5
    half = HEAD_DIM // 2
    frequency = ROPE_BASE ** (-np.arange(half).astype(np.float64) * 2.0 / HEAD_DIM)
    frequency = jnp.asarray(np.concatenate([frequency, frequency])[None, :].astype(np.float32))
    lane_blocks = rows // 128
    assert blocks_dev <= 128
    anywhere = pl.BlockSpec(memory_space=pl.ANY)
    vmem = pl.BlockSpec(memory_space=pltpu.VMEM)
    kv_stage_copies = sum(3 << s for s in range(chip_bits)) + chips
    assert tps >= 4
    bf16, f32 = jnp.bfloat16, jnp.float32
    dma = pltpu.SemaphoreType.DMA
    delta, k_rows, v_rows = pl.pallas_call(
        functools.partial(sublayer_kernel, seqs, tps, long_rows),
        out_shape=(jax.ShapeDtypeStruct((rows, width), bf16),) * 3,
        in_specs=[anywhere, anywhere, anywhere, vmem, vmem, vmem, vmem],
        out_specs=(vmem, vmem, vmem),
        scratch_shapes=[
            pltpu.VMEM(w_qkv.shape, bf16),
            pltpu.VMEM(w_out.shape, bf16),
            pltpu.VMEM((tps, rows, width), bf16),
            pltpu.VMEM((rows, width), bf16),
            pltpu.VMEM((2, chips, rows, 2 * width), bf16),
            pltpu.VMEM((heads, 1, rows), f32),
            pltpu.VMEM((heads, 1, rows), f32),
            pltpu.VMEM((heads, HEAD_DIM, rows), f32),
            pltpu.VMEM((width, rows), bf16),
            pltpu.VMEM((tps, rows, width), f32),
            pltpu.VMEM((tps, rows, width), bf16),
            pltpu.VMEM((tps, rows, width), bf16),
            pltpu.VMEM((tps, rows, width), bf16),
            pltpu.VMEM((seqs, lane_blocks, 128), jnp.int32),
            pltpu.VMEM((rows, HEAD_DIM), f32),
            pltpu.VMEM((rows, HEAD_DIM), f32),
            pltpu.VMEM((rows, 2 * width), f32),
            pltpu.VMEM(w_out.shape, bf16),
            pltpu.VMEM((width, rows), bf16),
            pltpu.VMEM((seqs, 128, 2 * width), bf16),
            pltpu.VMEM((seqs, 128, 2 * width), bf16),
            pltpu.VMEM((seqs, 1, 128), jnp.int32),
            pltpu.VMEM((seqs, 1, 128), jnp.int32),
            dma((2, tps, chunks)), dma((2, tps, chunks)),
            dma((chunks, kv_stage_copies)), dma((chunks, kv_stage_copies)),
            dma((chip_bits + 1,)), dma((chip_bits + 1,)),
            dma((tps, steps)), dma((2, tps, steps)),
            dma((2, seqs)), dma((2, seqs)),
            dma((7,)), dma((7,)),
            dma((3,)),
        ],
        compiler_params=pltpu.CompilerParams(
            collective_id=0, has_side_effects=True, vmem_limit_bytes=60 * 1024 * 1024),
    )(hidden, w_qkv, w_out, frequency, seg_ids.reshape(lane_blocks, 128), positions.reshape(lane_blocks, 128),
      jnp.pad(page_table, (0, 128 - blocks_dev)).reshape(1, 128))
    return (delta, k_rows.reshape(blocks_dev, PAGE, width), v_rows.reshape(blocks_dev, PAGE, width))


def solution(mesh):
    in_specs = (P("seq", "tp"), P(None, None, "tp"), P("tp", None), P("seq"), P("seq"), P("seq"))
    out_specs = (P("seq", "tp"), P("seq", None, "tp"), P("seq", None, "tp"))
    return jax.shard_map(
        functools.partial(body, mesh.shape["seq"], mesh.shape["tp"]),
        mesh=mesh, in_specs=in_specs, out_specs=out_specs, check_vma=False)
```

```python
import functools
import math

import jax
import jax.numpy as jnp
import numpy as np
from jax import lax
from jax.sharding import PartitionSpec as P
from jax.experimental import pallas as pl
from jax.experimental.pallas import tpu as pltpu

HEAD_DIM = 128
PAGE = 16
ROPE_BASE = 10000.0
EPSILON = 1e-05
NEG_LARGE = -1e30
SCALE = HEAD_DIM ** -0.5 * math.log2(math.e)
MESH = pl.DeviceIdType.MESH
CHUNK = 128
STRADDLE = 128


def row_sizes(rows):
    return [64] + [128] * (rows // 128 - 1) + [64]


def flip(index, bit):
    return index + (1 << bit) * (1 - 2 * ((index // (1 << bit)) % 2))


def flips(index, bits):
    found = [index]
    for bit in bits:
        found = found + [flip(one, bit) for one in found]
    return found


def sublayer_kernel(seqs, tps, long_rows,
                    hid, wqkv, wout, frequency, segments, positions, table,
                    delta, k_cache, v_cache,
                    wq_s, wo_s, hfull, q_s, kv, m_s, l_s, acc_s, att_s, part, sendbuf, from_left, from_right,
                    ints_all, cos2, sin2, paged, wo_end, att_end, sorted_rows, arrived, labels, labels_in,
                    z_send, z_recv, kv_send, kv_recv, int_send, int_recv, rs_send, rs_recv, page_send, page_recv, end_send, end_recv, local_sem):
    me = lax.axis_index("seq")
    z = lax.axis_index("tp")
    core, chip = me % 2, me // 2
    chips = seqs // 2
    chip_bits = chips.bit_length() - 1
    rows_dev, width = hid.shape
    heads = width // HEAD_DIM
    sizes = row_sizes(rows_dev)
    offsets = [sum(sizes[:c]) for c in range(len(sizes))]
    chunks = len(sizes)
    steps = rows_dev // CHUNK
    split = long_rows % rows_dev

    barrier = pltpu.get_barrier_semaphore()
    for ahead in range(1, seqs):
        pl.semaphore_signal(barrier, inc=1, device_id={"seq": lax.rem(me + ahead, seqs)}, device_id_type=MESH)

    @pl.when(z > 0)
    def _():
        pl.semaphore_signal(barrier, inc=1, device_id={"tp": z - 1}, device_id_type=MESH)

    @pl.when(z < tps - 1)
    def _():
        pl.semaphore_signal(barrier, inc=1, device_id={"tp": z + 1}, device_id_type=MESH)

    load_h = pltpu.make_async_copy(hid, hfull.at[z], local_sem.at[0])
    load_q = pltpu.make_async_copy(wqkv, wq_s, local_sem.at[1])
    load_o = pltpu.make_async_copy(wout, wo_s, local_sem.at[2])
    load_h.start()
    load_q.start()
    load_o.start()
    neighbours = (z > 0).astype(jnp.int32) + (z < tps - 1).astype(jnp.int32)
    pl.semaphore_wait(barrier, seqs - 1 + neighbours)

    def chunk_rows(c):
        return pl.ds(offsets[c], sizes[c])

    def z_copy(way, hop, c):
        shard = z - way * (hop - 1)
        source = hid.at[chunk_rows(c)] if hop == 1 else hfull.at[shard, chunk_rows(c)]
        side = 0 if way > 0 else 1
        return pltpu.make_async_remote_copy(
            src_ref=source, dst_ref=hfull.at[shard, chunk_rows(c)],
            send_sem=z_send.at[side, hop, c], recv_sem=z_recv.at[side, hop, c],
            device_id={"tp": z + way}, device_id_type=MESH)

    def has(way, hop):
        ahead = z + 1 < tps if way > 0 else z > 0
        held = z - (hop - 1) >= 0 if way > 0 else z + (hop - 1) < tps
        return ahead & held

    def gets(way, hop):
        return z - hop >= 0 if way > 0 else z + hop < tps

    def z_start(way, hop, c):
        @pl.when(has(way, hop))
        def _():
            z_copy(way, hop, c).start()

    def z_arrive(way, hop, c):
        @pl.when(gets(way, hop))
        def _():
            z_copy(way, hop, c).wait_recv()

    def z_pass(hop, c):
        for way in (1, -1):
            z_arrive(way, hop, c)
            if hop + 1 < tps:
                z_start(way, hop + 1, c)

    capacity = -(-(rows_dev // PAGE) // seqs)
    used = capacity * PAGE
    ascending, descending = tuple(range(chip_bits)), tuple(range(chip_bits))[::-1]
    routes = ((0, ascending, 0), (0, descending, 1), (1, descending, None))

    def useful(shard, reached, rest, low_bit):
        farthest = reached
        for bit in rest:
            farthest = farthest + (1 << bit) * (1 - (reached // (1 << bit)) % 2)
        good = farthest > shard
        return good if low_bit is None else good & (shard % 2 == low_bit)

    def kv_copies(stage, c):
        found = []
        if stage == chip_bits:
            for k in range(chips):
                shard = lax.rem(chip + k, chips)
                needed = None if k == 0 else shard < chip
                found.append((k == 0, needed, needed, kv.at[core, shard, chunk_rows(c)], flip(me, 0)))
        else:
            for side, order, low_bit in routes:
                half = sizes[c] // 2
                rows = pl.ds(offsets[c] + side * half, half)
                partner = flip(chip, order[stage])
                mine, theirs = flips(chip, order[:stage]), flips(partner, order[:stage])
                for k, (shard, other) in enumerate(zip(mine, theirs)):
                    found.append((k == 0, useful(shard, partner, order[stage + 1:], low_bit),
                                  useful(other, chip, order[stage + 1:], low_bit),
                                  kv.at[core, shard, rows], partner * 2 + core))
        base = sum(len(routes) << s for s in range(stage))
        return [
            (own, sends, receives, pltpu.make_async_remote_copy(
                src_ref=ref, dst_ref=ref, send_sem=kv_send.at[c, base + k], recv_sem=kv_recv.at[c, base + k],
                device_id={"seq": to}, device_id_type=MESH))
            for k, (own, sends, receives, ref, to) in enumerate(found)
        ]

    def when(condition, act):
        if condition is None:
            act()
        else:
            pl.when(condition)(act)

    def kv_start(stage, c, own):
        for first, sends, _, copy in kv_copies(stage, c):
            if first == own:
                when(sends, copy.start)

    def kv_arrive(stage, c):
        for _, _, receives, copy in kv_copies(stage, c):
            when(receives, copy.wait_recv)

    for way in (1, -1):
        z_start(way, 1, 0)
    for way in (1, -1):
        z_start(way, 1, 1)

    lane_blocks = rows_dev // 128
    ints_all[me] = segments[...]

    def ints_copy(bit):
        first = (me // (1 << bit)) * (1 << bit)
        block = ints_all.at[pl.ds(first, 1 << bit)]
        return pltpu.make_async_remote_copy(
            src_ref=block, dst_ref=block, send_sem=int_send.at[bit], recv_sem=int_recv.at[bit],
            device_id={"seq": flip(me, bit)}, device_id_type=MESH)

    ints_copy(0).start()
    if used < 128:
        arrived[:, used:, :] = jnp.zeros((seqs, 128 - used, 2 * width), jnp.bfloat16)

    def down_columns(row):
        return jnp.transpose(jnp.broadcast_to(row.astype(jnp.float32), (128, 128)))

    turn = jnp.where(lax.broadcasted_iota(jnp.int32, (128, HEAD_DIM), 1) < HEAD_DIM // 2, -1.0, 1.0)
    for block in range(lane_blocks):
        angle = down_columns(positions[block:block + 1, :]) * frequency[...]
        cos2[block * 128:(block + 1) * 128, :] = jnp.cos(angle)
        sin2[block * 128:(block + 1) * 128, :] = jnp.sin(angle) * turn

    load_h.wait()
    load_q.wait()

    def project(c):
        rows = chunk_rows(c)
        pieces = [hfull[t, rows, :].astype(jnp.float32) for t in range(tps)]
        total = sum(jnp.sum(piece, axis=1, keepdims=True) for piece in pieces)
        mean = total * (1.0 / (tps * width))
        centred = [piece - mean for piece in pieces]
        spread = sum(jnp.sum(piece * piece, axis=1, keepdims=True) for piece in centred)
        factor = lax.rsqrt(spread * (1.0 / (tps * width)) + EPSILON)
        normed = jnp.concatenate([(piece * factor).astype(jnp.bfloat16) for piece in centred], axis=1)
        cos, sin = cos2[rows, :], sin2[rows, :]
        for which in range(3):
            projected = jnp.dot(normed, wq_s[which], preferred_element_type=jnp.float32)
            for h in range(heads):
                part_h = projected[:, h * HEAD_DIM:(h + 1) * HEAD_DIM]
                if which < 2:
                    part_h = part_h * cos + pltpu.roll(part_h, HEAD_DIM // 2, 1) * sin
                value = part_h.astype(jnp.bfloat16)
                if which == 0:
                    q_s[rows, h * HEAD_DIM:(h + 1) * HEAD_DIM] = value
                else:
                    at = (which - 1) * width + h * HEAD_DIM
                    kv[core, chip, rows, at:at + HEAD_DIM] = value

    def kv_next(stage, c):
        if 0 <= c < chunks:
            kv_arrive(stage, c)
            if stage < chip_bits:
                kv_start(stage + 1, c, False)

    is_end = (z == 0) | (z == tps - 1)
    is_helper = (z == 1) | (z == tps - 2)
    beside = jnp.where(z == 0, 1, tps - 2)
    half_rows = pl.ds(core * (width // 2), width // 2)
    pieces = 4

    def weights_copy(piece):
        size = width // 2 // pieces
        at = pl.ds(core * (width // 2) + piece * size, size)
        return pltpu.make_async_remote_copy(
            src_ref=wout.at[at], dst_ref=wo_end.at[at], send_sem=end_send.at[3 + piece], recv_sem=end_recv.at[3 + piece],
            device_id={"tp": beside}, device_id_type=MESH)

    weights_share = pltpu.make_async_remote_copy(
        src_ref=wo_end.at[half_rows], dst_ref=wo_end.at[half_rows], send_sem=end_send.at[2], recv_sem=end_recv.at[2],
        device_id={"seq": flip(me, 0)}, device_id_type=MESH)

    for c in range(chunks):
        if c + 2 < chunks:
            for way in (1, -1):
                z_start(way, 1, c + 2)
        for piece in range(c * pieces // (chunks - 2), min((c + 1) * pieces // (chunks - 2), pieces)):
            pl.when(is_end)(weights_copy(piece).start)
        for hop in range(1, tps):
            z_pass(hop, c)
        if c <= chip_bits:
            ints_copy(c).wait()
            if c < chip_bits:
                ints_copy(c + 1).start()
        project(c)
        for stage in range(chip_bits + 1):
            kv_start(stage, c, True)
        kv_next(0, c - 1)
        for stage in range(1, chip_bits):
            kv_next(stage, c - 1 - stage)
        kv_next(chip_bits, c - chip_bits)

    if chunks <= chip_bits:
        for bit in range(chunks, chip_bits + 1):
            ints_copy(bit).wait()
            if bit < chip_bits:
                ints_copy(bit + 1).start()

    tiles = [(0, split), (split, rows_dev)] if split else [(0, rows_dev)]

    def seg_row(device):
        return [ints_all[device, r:r + 1, :] for r in range(lane_blocks)]

    def as_column(row):
        return down_columns(row)[:, :1]

    def score(key_at, h, tile):
        low, high = tile
        return lax.dot_general(kv[key_at + (pl.ds(h * HEAD_DIM, HEAD_DIM),)],
                               q_s[low:high, h * HEAD_DIM:(h + 1) * HEAD_DIM], (((1,), (1,)), ((), ())),
                               preferred_element_type=jnp.float32)

    def absorb(s, key_at, h, tile, mask, first):
        low, high = tile
        values = kv[key_at + (pl.ds(width + h * HEAD_DIM, HEAD_DIM),)]
        if mask is not None:
            s = jnp.where(mask, s, NEG_LARGE)
        top = jnp.max(s, axis=0, keepdims=True)
        if not first:
            before = m_s[h, :, low:high]
            top = jnp.maximum(top, before)
        p = jnp.exp2((s - top) * SCALE)
        total = jnp.sum(p, axis=0, keepdims=True)
        mixed = lax.dot_general(values, p.astype(jnp.bfloat16), (((0,), (0,)), ((), ())),
                                preferred_element_type=jnp.float32)
        if not first:
            alpha = jnp.exp2((before - top) * SCALE)
            total = total + alpha * l_s[h, :, low:high]
            mixed = mixed + alpha * acc_s[h, :, low:high]
        m_s[h, :, low:high] = top
        l_s[h, :, low:high] = total
        acc_s[h, :, low:high] = mixed

    def attend(units, mask=None, first=False):
        ahead = score(*units[0])
        for k, one in enumerate(units):
            now = ahead
            if k + 1 < len(units):
                ahead = score(*units[k + 1])
            absorb(now, *one, mask, first)

    own = seg_row(me)
    own_row = jnp.concatenate(own, axis=1).astype(jnp.float32)
    own_col = jnp.concatenate([as_column(row) for row in own], axis=0)
    starts_long = me * rows_dev < long_rows
    all_long = (me + 1) * rows_dev <= long_rows

    def attend_own(tile):
        low, high = tile
        key_index = lax.broadcasted_iota(jnp.int32, (high, high - low), 0)
        query_index = lax.broadcasted_iota(jnp.int32, (high, high - low), 1) + low
        mask = (own_col[:high] == own_row[:, low:high]) & (key_index <= query_index)
        attend([((core, chip, pl.ds(0, high)), h, tile) for h in range(heads)], mask, True)

    def attend_before(which, rows):
        tile = tiles[which]

        def attend_device(j, carry):
            attend([((j % 2, j // 2, rows), h, tile) for h in range(heads)])
            return carry

        lax.fori_loop(0, jnp.where(starts_long if which == 0 else all_long, me, 0), attend_device, 0)

    def attend_straddle():
        @pl.when(jnp.logical_not(starts_long))
        def _():
            before = me - 1
            row = ints_all[before, lane_blocks - 1:lane_blocks, :]
            low, high = tiles[0]
            mask = as_column(row) == own_row[:, low:high]
            at = (before % 2, before // 2, pl.ds(rows_dev - STRADDLE, STRADDLE))
            attend([(at, h, tiles[0]) for h in range(heads)], mask)

    def finish(tile):
        low, high = tile
        for h in range(heads):
            att_s[h * HEAD_DIM:(h + 1) * HEAD_DIM, low:high] = (
                acc_s[h, :, low:high] / l_s[h, :, low:high]).astype(jnp.bfloat16)

    def rs_copy(way, j, c):
        landing = from_left if way > 0 else from_right
        side = 0 if way > 0 else 1
        return pltpu.make_async_remote_copy(
            src_ref=sendbuf.at[j, step_rows(c)], dst_ref=landing.at[j, step_rows(c)],
            send_sem=rs_send.at[j, c], recv_sem=rs_recv.at[side, j, c],
            device_id={"tp": z + way}, device_id_type=MESH)

    ways = {1: list(range(tps - 1, 0, -1)), -1: list(range(0, tps - 1))}
    def step_rows(c):
        return pl.ds(c * CHUNK, CHUNK)

    def end_copy(which):
        low, high = tiles[which]
        there = att_end.at[:, low:high]
        return pltpu.make_async_remote_copy(
            src_ref=att_s.at[:, low:high], dst_ref=there, send_sem=end_send.at[which], recv_sem=end_recv.at[which],
            device_id={"tp": beside}, device_id_type=MESH)

    def project_out(tile):
        low, high = tile
        rows = pl.ds(low, high - low)

        def times(attended, weights, j):
            return lax.dot_general(
                attended[:, low:high], weights[:, j * width:(j + 1) * width], (((0,), (0,)), ((), ())),
                preferred_element_type=jnp.float32)

        @pl.when(is_helper)
        def _():
            for j in range(tps):
                part[j, rows, :] = times(att_s, wo_s, j) + times(att_end, wo_end, j)

        @pl.when(jnp.logical_not(is_helper | is_end))
        def _():
            for j in range(tps):
                part[j, rows, :] = times(att_s, wo_s, j)

        for way in (1, -1):
            @pl.when(z == (1 if way > 0 else tps - 2))
            def _():
                for j in ways[way]:
                    if (j > 1) if way > 0 else (j < tps - 2):
                        sendbuf[j, rows, :] = part[j, rows, :].astype(jnp.bfloat16)
                for c in range(low // CHUNK, high // CHUNK):
                    for j in ways[way]:
                        if (j > 1) if way > 0 else (j < tps - 2):
                            rs_copy(way, j, c).start()

    group = min(4, seqs)

    def page_copy(ahead, what):
        to, origin = lax.rem(me + ahead, seqs), me
        source, landing = (sorted_rows, arrived) if what == 0 else (labels, labels_in)
        if what == 0:
            source, landing = source.at[to, pl.ds(0, used)], landing.at[origin, pl.ds(0, used)]
        else:
            source, landing = source.at[to], landing.at[origin]
        return pltpu.make_async_remote_copy(
            src_ref=source, dst_ref=landing, send_sem=page_send.at[what, ahead], recv_sem=page_recv.at[what, ahead],
            device_id={"seq": to}, device_id_type=MESH)

    def sort_pages():
        blocks = rows_dev // PAGE
        lane = lax.broadcasted_iota(jnp.int32, (128, 128), 1)
        sub = lax.broadcasted_iota(jnp.int32, (128, 128), 0)
        page = table[...].astype(jnp.float32)
        owner = jnp.where(lane[:1] < blocks, jnp.floor((page + 0.5) * (1.0 / blocks)), -1.0)
        same = (down_columns(owner) == owner) & (sub < lane)
        rank = jnp.sum(jnp.where(same, 1.0, 0.0), axis=0, keepdims=True)
        within = page - owner * blocks
        which = lax.broadcasted_iota(jnp.int32, (16, 128), 0)
        facts = jnp.where(which == 0, owner, jnp.where(which == 1, rank, within)).astype(jnp.bfloat16)
        row = lax.broadcasted_iota(jnp.int32, (128, rows_dev), 1)
        to_rows = jnp.where(row // PAGE == lax.broadcasted_iota(jnp.int32, (128, rows_dev), 0), 1.0, 0.0)
        facts = jnp.dot(facts, to_rows.astype(jnp.bfloat16), preferred_element_type=jnp.float32)
        in_page = (lax.broadcasted_iota(jnp.int32, (1, rows_dev), 1) % PAGE).astype(jnp.float32)
        slot = facts[0:1] * 128.0 + facts[1:2] * PAGE + in_page
        which = lax.broadcasted_iota(jnp.int32, (16, rows_dev), 0)
        marks = jnp.where(which == 0, facts[2:3] + 1.0, in_page).astype(jnp.bfloat16)
        mine = kv[core, chip]
        for first in range(0, seqs, group):
            here = lax.broadcasted_iota(jnp.int32, (group * 128, rows_dev), 0) + first * 128
            pick = jnp.where(slot == here.astype(jnp.float32), 1.0, 0.0).astype(jnp.bfloat16)
            rows = jnp.dot(pick, mine, preferred_element_type=jnp.float32).astype(jnp.bfloat16)
            sorted_rows[first:first + group] = rows.reshape(group, 128, 2 * width)
            marked = lax.dot_general(marks, pick, (((1,), (1,)), ((), ())), preferred_element_type=jnp.float32)
            label = jnp.where(marked[0:1] > 0.0, (marked[0:1] - 1.0) * PAGE + marked[1:2] + 1.0, 0.0).astype(jnp.int32)
            for k in range(group):
                labels[first + k] = label[:, k * 128:(k + 1) * 128]

    def place_pages():
        for what in (0, 1):
            for ahead in range(1, seqs):
                page_copy(ahead, what).wait_recv()
        arrived[me, :used, :] = sorted_rows[me, :used, :]
        labels_in[me] = labels[me]
        paged[...] = jnp.zeros(paged.shape, jnp.float32)
        for first in range(0, seqs, group):
            label = jnp.concatenate([labels_in[first + k] for k in range(group)], axis=1)
            here = lax.broadcasted_iota(jnp.int32, (rows_dev, group * 128), 0) + 1
            pick = jnp.where(label == here, 1.0, 0.0).astype(jnp.bfloat16)
            rows = arrived[first:first + group].reshape(group * 128, 2 * width)
            paged[...] += jnp.dot(pick, rows, preferred_element_type=jnp.float32)

    last = chunks - 1
    early_rows = offsets[max(0, last - chip_bits + 1)]
    early, late = pl.ds(0, early_rows), pl.ds(early_rows, rows_dev - early_rows)
    work = [sort_pages, lambda: [attend_own(tile) for tile in tiles]]
    if early_rows:
        work += [functools.partial(attend_before, which, early) for which in range(len(tiles))]
    pending = [(c + min(stage + 1, chip_bits) + (stage == chip_bits) / 2, c, stage)
               for c in range(chunks) for stage in range(chip_bits + 1) if c + min(stage + 1, chip_bits) > last]
    pending = [(stage, c) for _, stage, c in sorted((slot, stage, c) for slot, c, stage in pending)]
    places = (0, 1, 2, 3)
    for k, one in enumerate(pending):
        for place, task in zip(places, work):
            if place == k:
                task()
        kv_next(*one)
    load_o.wait()

    @pl.when(is_helper)
    def _():
        for piece in range(pieces):
            weights_copy(piece).wait_recv()
        weights_share.start()

    for which, tile in enumerate(tiles):
        attend_before(which, late)
        if which == 0:
            attend_straddle()
        finish(tile)
        pl.when(is_end)(end_copy(which).start)

    for ahead in range(1, seqs):
        for what in (0, 1):
            page_copy(ahead, what).start()

    @pl.when(is_helper)
    def _():
        weights_share.wait()

    for which, tile in enumerate(tiles):
        pl.when(is_helper)(end_copy(which).wait_recv)
        project_out(tile)

    for c in range(steps):
        rows = step_rows(c)
        for hop in range(2, tps - 1):
            for way in (1, -1):
                landing = from_left if way > 0 else from_right

                @pl.when(z == (hop if way > 0 else tps - 1 - hop))
                def _():
                    for j in ways[way]:
                        if (j > hop) if way > 0 else (j < tps - 1 - hop):
                            rs_copy(way, j, c).wait_recv()
                            sendbuf[j, rows, :] = (
                                part[j, rows, :] + landing[j, rows, :].astype(jnp.float32)).astype(jnp.bfloat16)
                            rs_copy(way, j, c).start()

        if c == steps - 1:
            place_pages()

        @pl.when(z == 0)
        def _():
            rs_copy(-1, 0, c).wait_recv()
            delta[rows, :] = from_right[0, rows, :]

        @pl.when(z == tps - 1)
        def _():
            rs_copy(1, tps - 1, c).wait_recv()
            delta[rows, :] = from_left[tps - 1, rows, :]

        @pl.when((z > 1) & (z < tps - 1))
        def _():
            rs_copy(1, z, c).wait_recv()
            part[z, rows, :] = part[z, rows, :] + from_left[z, rows, :].astype(jnp.float32)

        @pl.when((z > 0) & (z < tps - 2))
        def _():
            rs_copy(-1, z, c).wait_recv()
            part[z, rows, :] = part[z, rows, :] + from_right[z, rows, :].astype(jnp.float32)

        @pl.when(jnp.logical_not(is_end))
        def _():
            delta[rows, :] = part[z, rows, :].astype(jnp.bfloat16)

    k_cache[...] = paged[:, :width].astype(jnp.bfloat16)
    v_cache[...] = paged[:, width:].astype(jnp.bfloat16)

    for piece in range(pieces):
        pl.when(is_end)(weights_copy(piece).wait_send)
    for which in range(len(tiles)):
        pl.when(is_end)(end_copy(which).wait_send)
    for ahead in range(1, seqs):
        for what in (0, 1):
            page_copy(ahead, what).wait_send()
    for c in range(chunks):
        for way in (1, -1):
            for hop in range(1, tps):
                @pl.when(has(way, hop))
                def _():
                    z_copy(way, hop, c).wait_send()
        for stage in range(chip_bits + 1):
            for _, sends, _, copy in kv_copies(stage, c):
                when(sends, copy.wait_send)
    for c in range(steps):
        for j in range(tps):
            @pl.when((z != j) & jnp.logical_not(is_end))
            def _():
                rs_copy(1, j, c).wait_send()


def body(seqs, tps, hidden, w_qkv, w_out, seg_ids, positions, page_table):
    rows, width = hidden.shape
    heads = width // HEAD_DIM
    chips = seqs // 2
    chip_bits = chips.bit_length() - 1
    chunks = len(row_sizes(rows))
    steps = rows // CHUNK
    blocks_dev = page_table.shape[0]
    long_rows = seqs * rows * 4 // 5
    half = HEAD_DIM // 2
    frequency = ROPE_BASE ** (-np.arange(half).astype(np.float64) * 2.0 / HEAD_DIM)
    frequency = jnp.asarray(np.concatenate([frequency, frequency])[None, :].astype(np.float32))
    lane_blocks = rows // 128
    assert blocks_dev <= 128
    anywhere = pl.BlockSpec(memory_space=pl.ANY)
    vmem = pl.BlockSpec(memory_space=pltpu.VMEM)
    kv_stage_copies = sum(3 << s for s in range(chip_bits)) + chips
    assert tps >= 4
    bf16, f32 = jnp.bfloat16, jnp.float32
    dma = pltpu.SemaphoreType.DMA
    delta, k_rows, v_rows = pl.pallas_call(
        functools.partial(sublayer_kernel, seqs, tps, long_rows),
        out_shape=(jax.ShapeDtypeStruct((rows, width), bf16),) * 3,
        in_specs=[anywhere, anywhere, anywhere, vmem, vmem, vmem, vmem],
        out_specs=(vmem, vmem, vmem),
        scratch_shapes=[
            pltpu.VMEM(w_qkv.shape, bf16),
            pltpu.VMEM(w_out.shape, bf16),
            pltpu.VMEM((tps, rows, width), bf16),
            pltpu.VMEM((rows, width), bf16),
            pltpu.VMEM((2, chips, rows, 2 * width), bf16),
            pltpu.VMEM((heads, 1, rows), f32),
            pltpu.VMEM((heads, 1, rows), f32),
            pltpu.VMEM((heads, HEAD_DIM, rows), f32),
            pltpu.VMEM((width, rows), bf16),
            pltpu.VMEM((tps, rows, width), f32),
            pltpu.VMEM((tps, rows, width), bf16),
            pltpu.VMEM((tps, rows, width), bf16),
            pltpu.VMEM((tps, rows, width), bf16),
            pltpu.VMEM((seqs, lane_blocks, 128), jnp.int32),
            pltpu.VMEM((rows, HEAD_DIM), f32),
            pltpu.VMEM((rows, HEAD_DIM), f32),
            pltpu.VMEM((rows, 2 * width), f32),
            pltpu.VMEM(w_out.shape, bf16),
            pltpu.VMEM((width, rows), bf16),
            pltpu.VMEM((seqs, 128, 2 * width), bf16),
            pltpu.VMEM((seqs, 128, 2 * width), bf16),
            pltpu.VMEM((seqs, 1, 128), jnp.int32),
            pltpu.VMEM((seqs, 1, 128), jnp.int32),
            dma((2, tps, chunks)), dma((2, tps, chunks)),
            dma((chunks, kv_stage_copies)), dma((chunks, kv_stage_copies)),
            dma((chip_bits + 1,)), dma((chip_bits + 1,)),
            dma((tps, steps)), dma((2, tps, steps)),
            dma((2, seqs)), dma((2, seqs)),
            dma((7,)), dma((7,)),
            dma((3,)),
        ],
        compiler_params=pltpu.CompilerParams(
            collective_id=0, has_side_effects=True, vmem_limit_bytes=60 * 1024 * 1024),
    )(hidden, w_qkv, w_out, frequency, seg_ids.reshape(lane_blocks, 128), positions.reshape(lane_blocks, 128),
      jnp.pad(page_table, (0, 128 - blocks_dev)).reshape(1, 128))
    return (delta, k_rows.reshape(blocks_dev, PAGE, width), v_rows.reshape(blocks_dev, PAGE, width))


def solution(mesh):
    in_specs = (P("seq", "tp"), P(None, None, "tp"), P("tp", None), P("seq"), P("seq"), P("seq"))
    out_specs = (P("seq", "tp"), P("seq", None, "tp"), P("seq", None, "tp"))
    return jax.shard_map(
        functools.partial(body, mesh.shape["seq"], mesh.shape["tp"]),
        mesh=mesh, in_specs=in_specs, out_specs=out_specs, check_vma=False)
```
